512 devices in a mesh: dp: 8 (over y, core), expert: 64 (over x, z).
Axes of the slice: x: 4, y: 4, z: 16, core: 2. Of those that a mesh axis runs over, the one named last changes fastest.
Arguments:
- tokens: bfloat16 [32768, 1024], P(('dp', 'expert')), may hold values from -6 to 6
- expert_ids: int32 [32768, 8], P(('dp', 'expert')), may hold values from 0 to 63, all different within a row; in each aligned block of 64 rows (0 to 63, 64 to 127, ...) at most 10 rows name the same one
- route_weight: float32 [32768, 8], P(('dp', 'expert')), may hold values from 0.05 to 0.5
- out_grad: bfloat16 [32768, 1024], P(('dp', 'expert')), may hold values from -6 to 6
- gate_weight: bfloat16 [64, 1024, 384], P('expert', 'dp'), may hold values from -0.1875 to 0.1875
- up_weight: bfloat16 [64, 1024, 384], P('expert', 'dp'), may hold values from -0.1875 to 0.1875
- down_weight: bfloat16 [64, 384, 1024], P('expert', None, 'dp'), may hold values from -0.3125 to 0.3125
Outputs:
- layer_out: bfloat16 [32768, 1024], P(('dp', 'expert'))
- token_grad: bfloat16 [32768, 1024], P(('dp', 'expert'))
- route_grad: float32 [32768, 8], P(('dp', 'expert'))
- gate_grad: float32 [64, 1024, 384], P('expert', 'dp')
- up_grad: float32 [64, 1024, 384], P('expert', 'dp')
- down_grad: float32 [64, 384, 1024], P('expert', None, 'dp')
The draws below stay inside these ranges and needn't reach their ends.
Inputs may be any that keep to these rules, and one draw needn't show every extreme that they name: `expert_ids`: each token names 8 different experts. Among the 64 tokens of one device no expert is named by more than 10 tokens, and in every draw some expert is named by exactly 10 tokens of some device.
All inputs are finite; a program needn't handle non-finite values.
Results may differ from the reference program's by a relative error of at most 0.012.
Values may be sent and summed in bfloat16 or wider, within the bound.
No kernel may reach another device: no remote copies, remote signals or barrier semaphores. Data moves between devices by JAX's collectives and lax.ppermute only.
A program may use at most 64 MiB of HBM per device.

```python
import math
import jax
import jax.numpy as jnp
import numpy as np
from jax import lax

D = 1024
HID = 384
TOP = 8
TOK_DEV = 64
EXPERTS = 64
CAP = 10
TOKENS = 32768
N_DP = 8
N_EXPERT = 64


def shard_levels(key, extent, shards, low, top_value):
    def one(axis_at, blocks):
        heights = jax.random.uniform(jax.random.fold_in(jax.random.fold_in(key, 6), axis_at), (blocks,), jnp.float32, low / len(shards), top_value / len(shards))
        return jnp.repeat(jnp.exp(heights), extent[axis_at] // blocks).reshape((-1,) + (1,) * (len(extent) - axis_at - 1))

    gain = one(*shards[0])
    for cut in shards[1:]:
        gain = gain * one(*cut)
    return gain


def shared_out(stream_key, own, number, rows, count, top, most, lean):
    ranking = jax.random.permutation(stream_key, count)
    heavy_load, ordinary = load_shares(count, rows * top, most, lean, True), load_shares(count, rows * top, most, lean, False)
    places = jnp.arange(count)

    def named(sizes, offset_by):
        used = int((sizes > 0).sum())
        fixed = max(1, used // 4)
        moved = fixed + (places - fixed + offset_by * (used - fixed)) % max(1, count - fixed)
        return jnp.zeros((count,), jnp.int32).at[ranking[jnp.where(places < fixed, places, moved)]].set(jnp.asarray(sizes, jnp.int32))

    sizes = jnp.where(number % 4 == 0, named(heavy_load, number // 4), named(ordinary, number - number // 4 - 1))
    mixed = jax.random.permutation(jax.random.fold_in(own, 3), count)
    source_of, taker = mixed[0:count // 2 * 2:2], mixed[1:count // 2 * 2:2]
    slack = jnp.minimum(sizes[source_of] - 1, most - sizes[taker]) // 2
    slack = jnp.where((source_of == ranking[0]) | (taker == ranking[0]) | (sizes[taker] == 0), 0, jnp.maximum(slack, 0))
    moved = jax.random.randint(jax.random.fold_in(own, 4), (count // 2,), 0, 1 << 20) % (slack + 1)
    sizes = sizes.at[source_of].add(-moved).at[taker].add(moved)
    labels = jnp.searchsorted(jnp.cumsum(sizes), jnp.arange(rows * top), side="right").astype(jnp.int32)
    listing = labels.reshape(top, rows).T
    listing = listing[jax.random.permutation(jax.random.fold_in(own, 1), rows)]
    offset_by = jax.random.randint(jax.random.fold_in(own, 2), (rows, 1), 0, top)
    return jnp.take_along_axis(listing, (jnp.arange(top)[None, :] + offset_by) % top, axis=1)


def load_shares(number_of, total, limit, lean, full):
    portions = [(1 << 20) // math.isqrt(rank ** lean) + 1 for rank in range(1, number_of + 1)]
    largest = limit if full else min(limit, max(-(-total // number_of), total * portions[0] // sum(portions)))
    least = 1 if total - largest >= number_of - 1 else 0
    given, spare = [largest] + [least] * (number_of - 1), total - largest - least * (number_of - 1)
    while spare > 0:
        movable = [i for i in range(1, number_of) if given[i] < largest] or [i for i in range(1, number_of) if given[i] < limit]
        pool, left = sum([portions[i] for i in movable]), spare
        for i in movable:
            more = min(limit - given[i], max(1, left * portions[i] // pool), spare)
            given[i] = given[i] + more
            spare = spare - more
    return np.array(given)


def gaussian(key, dims, scale, limit, split=(), kind=jnp.bfloat16):
    loudness = shard_levels(key, dims, split, -0.22, 0.18) if split else 1.0
    entries = jax.random.normal(key, dims, jnp.float32) * scale * loudness
    return jnp.minimum(jnp.maximum(entries, -limit), limit).astype(kind)


def setup_inputs(seed: int = 0) -> dict:
    key_list = jax.random.split(jax.random.key(seed), 8)
    tokens = gaussian(key_list[0], (TOKENS, D), 1.0, 6.0, ((0, 512),))
    expert_ids_keys = jax.random.split(jax.random.fold_in(key_list[1], 1), TOKENS // TOK_DEV)
    expert_ids_turns = jax.random.permutation(jax.random.fold_in(key_list[1], 3), TOKENS // TOK_DEV)
    expert_ids = jax.vmap(lambda own, number: shared_out(jax.random.fold_in(key_list[1], 2), own, number, TOK_DEV, EXPERTS, TOP, CAP, 1))(expert_ids_keys, expert_ids_turns).reshape((TOKENS, TOP))
    route_weight = jnp.clip(jnp.exp(math.log(0.5) - 2.3025851 * jax.random.uniform(key_list[2], (TOKENS, TOP), jnp.float32) ** shard_levels(key_list[2], (TOKENS, TOP), ((0, 512),), -0.2, 0.2)), 0.05, 0.5)
    out_grad = gaussian(key_list[3], (TOKENS, D), 1.0, 6.0, ((0, 512),))
    gate_weight = gaussian(key_list[4], (EXPERTS, D, HID), D ** -0.5, 0.1875, ((0, 64), (1, 8)))
    up_weight = gaussian(key_list[5], (EXPERTS, D, HID), D ** -0.5, 0.1875, ((0, 64), (1, 8)))
    down_weight = gaussian(key_list[6], (EXPERTS, HID, D), HID ** -0.5, 0.3125, ((0, 64), (2, 8)))
    return {"tokens": tokens, "expert_ids": expert_ids, "route_weight": route_weight, "out_grad": out_grad, "gate_weight": gate_weight, "up_weight": up_weight, "down_weight": down_weight}


def expert_pass(x_rows, dy_rows, gate_w, up_w, down_w):
    gate_act = jnp.dot(x_rows, gate_w, preferred_element_type=jnp.float32)
    up_act = jnp.dot(x_rows, up_w, preferred_element_type=jnp.float32)
    sigmoid_g = jax.nn.sigmoid(gate_act)
    hidden = (gate_act * sigmoid_g * up_act).astype(jnp.bfloat16)
    y_rows = jnp.dot(hidden, down_w, preferred_element_type=jnp.float32).astype(jnp.bfloat16)
    hidden_grad = jnp.dot(dy_rows, down_w.T, preferred_element_type=jnp.float32)
    gate_back = (hidden_grad * up_act * sigmoid_g * (1.0 + gate_act * (1.0 - sigmoid_g))).astype(jnp.bfloat16)
    up_back = (hidden_grad * gate_act * sigmoid_g).astype(jnp.bfloat16)
    x_grad = (jnp.dot(gate_back, gate_w.T, preferred_element_type=jnp.float32)
              + jnp.dot(up_back, up_w.T, preferred_element_type=jnp.float32)).astype(jnp.bfloat16)
    gate_part = jnp.dot(x_rows.T, gate_back, preferred_element_type=jnp.float32).astype(jnp.bfloat16)
    up_part = jnp.dot(x_rows.T, up_back, preferred_element_type=jnp.float32).astype(jnp.bfloat16)
    down_part = jnp.dot(hidden.T, dy_rows, preferred_element_type=jnp.float32).astype(jnp.bfloat16)
    return y_rows, x_grad, gate_part, up_part, down_part


def reference(tokens, expert_ids, route_weight, out_grad, gate_weight, up_weight, down_weight):
    group_rows = TOK_DEV * N_EXPERT
    max_rows = N_EXPERT * CAP
    x_groups = tokens.reshape(N_DP, group_rows, D)
    id_groups = expert_ids.reshape(N_DP, group_rows, TOP)
    weight_groups = route_weight.reshape(N_DP, group_rows, TOP)
    grad_groups = out_grad.reshape(N_DP, group_rows, D)

    def per_group(carry, group):
        x_part, id_part, weight_part, grad_part = group
        flat_ids = id_part.reshape(-1).astype(jnp.int32)
        one_hot = (flat_ids[:, None] == jnp.arange(EXPERTS, dtype=jnp.int32)[None, :]).astype(jnp.int32)
        slot_rank = jnp.sum((jnp.cumsum(one_hot, 0) - one_hot) * one_hot, 1).astype(jnp.int32)
        pair_slots = (flat_ids * max_rows + slot_rank).astype(jnp.int32)
        x_pairs = jnp.repeat(x_part, TOP, 0)
        dy_pairs = (weight_part.reshape(-1, 1) * jnp.repeat(grad_part, TOP, 0).astype(jnp.float32)).astype(jnp.bfloat16)
        x_buffer = jnp.zeros((EXPERTS * max_rows, D), jnp.bfloat16).at[pair_slots].set(x_pairs)
        dy_buffer = jnp.zeros((EXPERTS * max_rows, D), jnp.bfloat16).at[pair_slots].set(dy_pairs)
        x_buffer = x_buffer.reshape(EXPERTS, max_rows, D)
        dy_buffer = dy_buffer.reshape(EXPERTS, max_rows, D)

        def per_expert(items):
            return expert_pass(*items)

        y_buf, dx_buf, gate_part, up_part, down_part = lax.map(
            per_expert, (x_buffer, dy_buffer, gate_weight, up_weight, down_weight))
        y_pairs = y_buf.reshape(-1, D)[pair_slots].reshape(group_rows, TOP, D)
        dx_pairs = dx_buf.reshape(-1, D)[pair_slots].reshape(group_rows, TOP, D)
        layer_part = jnp.sum(weight_part[:, :, None] * y_pairs.astype(jnp.float32), 1).astype(jnp.bfloat16)
        route_part = jnp.sum(grad_part.astype(jnp.float32)[:, None, :] * y_pairs.astype(jnp.float32), 2)
        token_part = jnp.sum(dx_pairs.astype(jnp.float32), 1).astype(jnp.bfloat16)
        new_carry = (carry[0] + gate_part.astype(jnp.float32),
                     carry[1] + up_part.astype(jnp.float32),
                     carry[2] + down_part.astype(jnp.float32))
        return new_carry, (layer_part, token_part, route_part)

    start_carry = (jnp.zeros((EXPERTS, D, HID), jnp.float32),
                   jnp.zeros((EXPERTS, D, HID), jnp.float32),
                   jnp.zeros((EXPERTS, HID, D), jnp.float32))
    grads, stacked = lax.scan(per_group, start_carry, (x_groups, id_groups, weight_groups, grad_groups))
    layer_out = stacked[0].reshape(TOKENS, D)
    token_grad = stacked[1].reshape(TOKENS, D)
    route_grad = stacked[2].reshape(TOKENS, TOP)
    return (layer_out, token_grad, route_grad, grads[0], grads[1], grads[2])
```

```python
import jax
import jax.numpy as jnp
from jax import lax
from jax.experimental import pallas as pl
from jax.experimental.pallas import tpu as pltpu
from jax.sharding import Mesh
from jax.sharding import PartitionSpec as P

BF = jnp.bfloat16
F32 = jnp.float32
NX, NZ, NDP = 4, 16, 8
CAP = 10
SLOTS = NZ * CAP
AUX = 128


def dot(a, b, ca, cb):
    return lax.dot_general(a, b, (((ca,), (cb,)), ((), ())), preferred_element_type=F32)


def moe_kernel(col_ref, pos_ref, w_ref, xd_ref, wt_ref, grad_ref, part_ref, sel_all, rows_all):
    e = pl.program_id(0)
    tok = xd_ref.shape[0]
    feat = (xd_ref.shape[1] - AUX) // 2
    hid = wt_ref.shape[3] // 3
    picked = pos_ref[0] == lax.broadcasted_iota(jnp.int32, (SLOTS, tok), 0)
    sel = jnp.where(picked, 1.0, 0.0).astype(BF)
    w = jnp.sum(jnp.where(picked, w_ref[0], 0.0), axis=1, keepdims=True)
    xe = dot(sel, xd_ref[:, :feat], 1, 0).astype(BF)
    de = dot(sel, xd_ref[:, feat + AUX :], 1, 0).astype(BF)
    wt = wt_ref[:, 0].reshape(feat, 3 * hid)
    gu = dot(xe, wt[:, : 2 * hid], 1, 0)
    hd = dot(de, wt[:, 2 * hid :], 1, 0)
    g = gu[:, :hid]
    u = gu[:, hid:]
    s = jax.nn.sigmoid(g)
    gs = g * s
    h = gs * u
    rg = jnp.sum(h * hd, axis=1, keepdims=True)
    wh = (w * h).astype(BF)
    hg = w * hd
    gb = (hg * u * s * (1.0 + g * (1.0 - s))).astype(BF)
    ub = (hg * gs).astype(BF)
    act = jnp.concatenate([gb, ub], axis=1)
    base = pl.multiple_of(e * SLOTS, SLOTS)
    here = pl.ds(base, SLOTS)
    sel_all[here, :] = sel
    rows_all[here, :feat] = dot(wh, wt[:, 2 * hid :], 1, 1).astype(BF)
    rows_all[here, feat + AUX :] = dot(act, wt[:, : 2 * hid], 1, 1).astype(BF)
    lane = lax.broadcasted_iota(jnp.int32, (SLOTS, AUX), 1)
    mine = col_ref[0] + e
    rg_hi = rg.astype(BF).astype(F32)
    aux = jnp.where(lane == mine, rg_hi, 0.0) + jnp.where(lane == mine + AUX // 2, rg - rg_hi, 0.0)
    rows_all[here, feat : feat + AUX] = aux.astype(BF)
    grad_ref[:, 0, :, : 2 * hid] = dot(xe, act, 0, 0).astype(BF).reshape(NDP, feat // NDP, 2 * hid)
    grad_ref[:, 0, :, 2 * hid :] = dot(de, wh, 0, 0).astype(BF).reshape(NDP, feat // NDP, hid)

    @pl.when(e == NX - 1)
    def _():
        for lo in range(0, 2 * feat + AUX, 544):
            part_ref[:, lo : lo + 544] = dot(
                sel_all[...], rows_all[:, lo : lo + 544], 0, 0
            ).astype(BF)


def experts(col, pos, w, xd, wt):
    tok, width = xd.shape
    feat = (width - AUX) // 2
    hid3 = wt.shape[3]
    rows = feat // NDP
    slots = NX * SLOTS
    flops = 2 * slots * (tok * width * 2 + 9 * feat * hid3 // 3)
    return pl.pallas_call(
        moe_kernel,
        grid_spec=pltpu.PrefetchScalarGridSpec(
            num_scalar_prefetch=1,
            grid=(NX,),
            in_specs=[
                pl.BlockSpec((1, 1, tok), lambda e, c: (e, 0, 0)),
                pl.BlockSpec((1, 1, tok), lambda e, c: (e, 0, 0)),
                pl.BlockSpec((tok, width), lambda e, c: (0, 0)),
                pl.BlockSpec((NDP, 1, rows, hid3), lambda e, c: (0, e, 0, 0)),
            ],
            out_specs=[
                pl.BlockSpec((NDP, 1, rows, hid3), lambda e, c: (0, e, 0, 0)),
                pl.BlockSpec((tok, width), lambda e, c: (0, 0)),
            ],
            scratch_shapes=[
                pltpu.VMEM((slots, tok), BF),
                pltpu.VMEM((slots, width), BF),
            ],
        ),
        out_shape=[
            jax.ShapeDtypeStruct((NDP, NX, rows, hid3), BF),
            jax.ShapeDtypeStruct((tok, width), BF),
        ],
        cost_estimate=pl.CostEstimate(
            flops=flops, bytes_accessed=30_000_000, transcendentals=slots * hid3 // 3
        ),
    )(col, pos, w, xd, wt)


def shift(value, step):
    return lax.ppermute(value, "z", [(i, (i + step) % NZ) for i in range(NZ)])


def add(a, b):
    return (a.astype(F32) + b.astype(F32)).astype(BF)


def shards(tokens, expert_ids, route_weight, out_grad, gate_weight, up_weight, down_weight):
    rows, feat = tokens.shape
    hid = gate_weight.shape[2]
    z = lax.axis_index("z")
    half = AUX // 2
    wl = jnp.concatenate([gate_weight[0], up_weight[0], down_weight[0].T], axis=1)
    wa = lax.all_gather(wl, ("y", "c", "x"), axis=0, tiled=True)
    place = (expert_ids % NZ) * NX + expert_ids // NZ
    hot = place[:, :, None] == jnp.arange(half, dtype=jnp.int32)
    dense = jnp.sum(jnp.where(hot, route_weight[:, :, None], 0.0), 1)
    hi = lax.reduce_precision(dense, 8, 7)
    pay = jnp.concatenate([tokens, hi.astype(BF), (dense - hi).astype(BF), out_grad], axis=1)
    blocks = [pay]
    right = left = pay
    for step in range(1, NZ // 2):
        right = shift(right, 1)
        left = shift(left, -1)
        blocks += [right, left]
    cut = feat + AUX
    blocks.append(jnp.concatenate([shift(right[:, :cut], 1), shift(left[:, cut:], -1)], axis=1))
    xd = jnp.concatenate(blocks, axis=0)
    wz = xd[:, feat : feat + half].astype(F32) + xd[:, feat + half : cut].astype(F32)
    wz = lax.dynamic_slice_in_dim(wz, z * NX, NX, 1).T
    live = wz > 0.0
    pos = jnp.where(live, jnp.cumsum(live.astype(jnp.int32), axis=1) - 1, -1)
    col = (z * NX).astype(jnp.int32).reshape(1)
    grads, part = experts(
        col, pos[:, None, :], wz[:, None, :], xd, wa.reshape(NDP, NX, feat // NDP, 3 * hid)
    )
    summed = lax.psum_scatter(
        grads.reshape(-1, 3 * hid), ("y", "c", "x"), scatter_dimension=0, tiled=True
    )

    def block(i):
        return part[i * rows : (i + 1) * rows]

    last = block(NZ - 1)
    toward_right = shift(last[:, :cut], 1)
    toward_left = shift(last[:, cut:], -1)
    far = block(2 * (NZ // 2 - 1))
    toward_right = jnp.concatenate([add(toward_right, far[:, :cut]), far[:, cut:]], axis=1)
    far = block(2 * (NZ // 2 - 1) - 1)
    toward_left = jnp.concatenate([far[:, :cut], add(toward_left, far[:, cut:])], axis=1)
    for step in range(NZ // 2 - 1, 0, -1):
        toward_right = shift(toward_right, 1)
        toward_left = shift(toward_left, -1)
        if step > 1:
            toward_right = add(toward_right, block(2 * (step - 1)))
            toward_left = add(toward_left, block(2 * (step - 1) - 1))
    total = (
        block(0).astype(F32) + toward_right.astype(F32) + toward_left.astype(F32)
    )
    layer_out = total[:, :feat].astype(BF)
    token_grad = total[:, cut:].astype(BF)
    pair = total[:, feat : feat + half] + total[:, feat + half : cut]
    route_grad = jnp.sum(jnp.where(hot, pair[:, None, :], 0.0), 2)
    summed = summed.astype(F32)
    gate_grad = summed[:, :hid][None]
    up_grad = summed[:, hid : 2 * hid][None]
    down_grad = summed[:, 2 * hid :].T[None]
    return layer_out, token_grad, route_grad, gate_grad, up_grad, down_grad


def solution(mesh):
    grid = Mesh(mesh.devices.reshape(-1, 2, NX, NZ), ("y", "c", "x", "z"))
    dp, ex = ("y", "c"), ("x", "z")
    rowwise = P(dp + ex, None)
    return jax.shard_map(
        shards,
        mesh=grid,
        in_specs=(rowwise, rowwise, rowwise, rowwise, P(ex, dp, None), P(ex, dp, None), P(ex, None, dp)),
        out_specs=(rowwise, rowwise, rowwise, P(ex, dp, None), P(ex, dp, None), P(ex, None, dp)),
        check_vma=False,
    )
```

```python
import jax
import jax.numpy as jnp
from jax import lax
from jax.experimental import pallas as pl
from jax.experimental.pallas import tpu as pltpu
from jax.sharding import Mesh
from jax.sharding import PartitionSpec as P

BF = jnp.bfloat16
F32 = jnp.float32
NX, NY, NZ, NC = 4, 4, 16, 2
NDP = NY * NC
HOPS = NZ // 2
CAP = 10
SLOTS = NZ * CAP
AUX = 128
PLANES = 8


def dot(a, b, ca, cb):
    return lax.dot_general(a, b, (((ca,), (cb,)), ((), ())), preferred_element_type=F32)


def moe_kernel(ids_ref, xa_ref, xb_ref, wt_ref, keep_ref, send_ref, pa_ref, pb_ref, pos_s, w_s, sel_s, rows_s):
    e = pl.program_id(0)
    col = ids_ref[0]
    core = ids_ref[1]
    tok = xa_ref.shape[0]
    feat = xb_ref.shape[1]
    hid = wt_ref.shape[3] // 3

    @pl.when(e == 0)
    def _():
        row = lax.broadcasted_iota(jnp.int32, (PLANES, AUX), 0)
        lane = lax.broadcasted_iota(jnp.int32, (PLANES, AUX), 1)
        want = (row < NX) & ((lane == col + row) | (lane == col + row + AUX // 2))
        w = dot(jnp.where(want, 1.0, 0.0).astype(BF), xa_ref[:, feat:], 1, 1)
        w_s[...] = w
        live = jnp.where(w > 0.0, 1.0, 0.0)
        r = lax.broadcasted_iota(jnp.int32, (128, 128), 0)
        c = lax.broadcasted_iota(jnp.int32, (128, 128), 1)
        upper = jnp.where(r <= c, 1.0, 0.0).astype(BF)
        before = jnp.full((PLANES, 1), -1.0, F32)
        for lo in range(0, tok, 128):
            part = live[:, lo : lo + 128]
            rank = dot(part.astype(BF), upper, 1, 0) + before
            pos_s[:, lo : lo + 128] = jnp.where(part > 0.0, rank, -1.0).astype(jnp.int32)
            before = before + jnp.sum(part, axis=1, keepdims=True)

    picked = pos_s[pl.ds(e, 1), :] == lax.broadcasted_iota(jnp.int32, (SLOTS, tok), 0)
    sel = jnp.where(picked, 1.0, 0.0).astype(BF)
    w = jnp.sum(jnp.where(picked, w_s[pl.ds(e, 1), :], 0.0), axis=1, keepdims=True)
    xe = dot(sel, xa_ref[:, :feat], 1, 0).astype(BF)
    de = dot(sel, xb_ref[...], 1, 0).astype(BF)
    wt = wt_ref[:, 0].reshape(feat, 3 * hid)
    gu = dot(xe, wt[:, : 2 * hid], 1, 0)
    hd = dot(de, wt[:, 2 * hid :], 1, 0)
    g = gu[:, :hid]
    u = gu[:, hid:]
    s = jax.nn.sigmoid(g)
    gs = g * s
    h = gs * u
    rg = jnp.sum(h * hd, axis=1, keepdims=True)
    wh = (w * h).astype(BF)
    hg = w * hd
    gb = (hg * u * s * (1.0 + g * (1.0 - s))).astype(BF)
    ub = (hg * gs).astype(BF)
    act = jnp.concatenate([gb, ub], axis=1)
    here = pl.ds(pl.multiple_of(e * SLOTS, SLOTS), SLOTS)
    sel_s[here, :] = sel
    rows_s[here, :feat] = dot(wh, wt[:, 2 * hid :], 1, 1).astype(BF)
    lane = lax.broadcasted_iota(jnp.int32, (SLOTS, AUX), 1)
    mine = col + e
    rg_hi = rg.astype(BF).astype(F32)
    aux = jnp.where(lane == mine, rg_hi, 0.0) + jnp.where(lane == mine + AUX // 2, rg - rg_hi, 0.0)
    rows_s[here, feat : feat + AUX] = aux.astype(BF)
    rows_s[here, feat + AUX :] = dot(act, wt[:, : 2 * hid], 1, 1).astype(BF)
    step = feat // NDP

    def halves(v):
        even = jnp.concatenate([v[:, i * step : (i + 1) * step] for i in range(0, NDP, 2)], axis=1)
        odd = jnp.concatenate([v[:, i * step : (i + 1) * step] for i in range(1, NDP, 2)], axis=1)
        return jnp.where(core == 0, even, odd), jnp.where(core == 0, odd, even)

    xk, xs = halves(xe)
    dk, ds = halves(de)
    keep_ref[:, 0, :, : 2 * hid] = dot(xk, act, 0, 0).astype(BF).reshape(NY, step, 2 * hid)
    keep_ref[:, 0, :, 2 * hid :] = dot(dk, wh, 0, 0).astype(BF).reshape(NY, step, hid)
    send_ref[:, 0, :, : 2 * hid] = dot(xs, act, 0, 0).astype(BF).reshape(NY, step, 2 * hid)
    send_ref[:, 0, :, 2 * hid :] = dot(ds, wh, 0, 0).astype(BF).reshape(NY, step, hid)

    @pl.when(e == NX - 1)
    def _():
        for lo in range(0, feat + AUX, 384):
            pa_ref[:, lo : lo + 384] = dot(sel_s[...], rows_s[:, lo : lo + 384], 0, 0).astype(BF)
        for lo in range(0, feat, 512):
            off = feat + AUX + lo
            pb_ref[:, lo : lo + 512] = dot(sel_s[...], rows_s[:, off : off + 512], 0, 0).astype(BF)


def experts(ids, xa, xb, wt):
    tok, feat = xb.shape
    hid3 = wt.shape[3]
    rows = feat // NDP
    slots = NX * SLOTS
    width = 2 * feat + AUX
    flops = 2 * slots * (tok * width * 2 + 9 * feat * hid3 // 3)
    whole = lambda e, s: (0, 0)
    return pl.pallas_call(
        moe_kernel,
        grid_spec=pltpu.PrefetchScalarGridSpec(
            num_scalar_prefetch=1,
            grid=(NX,),
            in_specs=[
                pl.BlockSpec((tok, feat + AUX), whole),
                pl.BlockSpec((tok, feat), whole),
                pl.BlockSpec((NDP, 1, rows, hid3), lambda e, s: (0, e, 0, 0)),
            ],
            out_specs=[
                pl.BlockSpec((NY, 1, rows, hid3), lambda e, s: (0, e, 0, 0)),
                pl.BlockSpec((NY, 1, rows, hid3), lambda e, s: (0, e, 0, 0)),
                pl.BlockSpec((tok, feat + AUX), whole),
                pl.BlockSpec((tok, feat), whole),
            ],
            scratch_shapes=[
                pltpu.VMEM((PLANES, tok), jnp.int32),
                pltpu.VMEM((PLANES, tok), F32),
                pltpu.VMEM((slots, tok), BF),
                pltpu.VMEM((slots, width), BF),
            ],
        ),
        out_shape=[
            jax.ShapeDtypeStruct((NY, NX, rows, hid3), BF),
            jax.ShapeDtypeStruct((NY, NX, rows, hid3), BF),
            jax.ShapeDtypeStruct((tok, feat + AUX), BF),
            jax.ShapeDtypeStruct((tok, feat), BF),
        ],
        cost_estimate=pl.CostEstimate(
            flops=flops, bytes_accessed=30_000_000, transcendentals=slots * hid3 // 3
        ),
    )(ids, xa, xb, wt)


def pack_kernel(g_ref, u_ref, d_ref, o_ref):
    hid = g_ref.shape[2]
    o_ref[:, :hid] = g_ref[0]
    o_ref[:, hid : 2 * hid] = u_ref[0]
    o_ref[:, 2 * hid :] = d_ref[0].astype(F32).T.astype(BF)


def pack(g, u, d):
    return pl.pallas_call(
        pack_kernel, out_shape=jax.ShapeDtypeStruct((g.shape[1], 3 * g.shape[2]), BF)
    )(g, u, d)


def unpack_kernel(s_ref, g_ref, u_ref, d_ref):
    hid = g_ref.shape[2]
    g_ref[0] = s_ref[:, :hid].astype(F32)
    u_ref[0] = s_ref[:, hid : 2 * hid].astype(F32)
    d_ref[0] = s_ref[:, 2 * hid :].astype(F32).T


def unpack(s):
    rows, hid = s.shape[0], s.shape[1] // 3
    return pl.pallas_call(
        unpack_kernel,
        out_shape=[
            jax.ShapeDtypeStruct((1, rows, hid), F32),
            jax.ShapeDtypeStruct((1, rows, hid), F32),
            jax.ShapeDtypeStruct((1, hid, rows), F32),
        ],
    )(s)


def around(value, sign):
    pairs = [(z, (z + sign) % NZ) for z in range(NZ)]
    pairs += [(NZ + z, NZ + (z - sign) % NZ) for z in range(NZ)]
    return lax.ppermute(value, ("c", "z"), pairs)


def swap(value):
    return lax.ppermute(value, "c", [(0, 1), (1, 0)])


def add(a, b):
    return (a.astype(F32) + b.astype(F32)).astype(BF)


def shards(tokens, expert_ids, route_weight, out_grad, gate_weight, up_weight, down_weight):
    rows, feat = tokens.shape
    hid = gate_weight.shape[2]
    z = lax.axis_index("z").astype(jnp.int32)
    core = lax.axis_index("c").astype(jnp.int32)
    half = AUX // 2
    pair_rows = 2 * rows
    wa = lax.all_gather(pack(gate_weight, up_weight, down_weight), ("y", "c", "x"), axis=0, tiled=True)
    place = (expert_ids % NZ) * NX + expert_ids // NZ
    hot = place[:, :, None] == jnp.arange(half, dtype=jnp.int32)
    dense = jnp.sum(jnp.where(hot, route_weight[:, :, None], 0.0), 1)
    hi = lax.reduce_precision(dense, 8, 7)
    own_a = jnp.concatenate([tokens, hi.astype(BF), (dense - hi).astype(BF)], axis=1)
    chain_a = chip_a = jnp.concatenate([own_a, swap(own_a)], axis=0)
    chain_b = chip_b = jnp.concatenate([out_grad, swap(out_grad)], axis=0)
    got_a, got_b = [], []
    for _ in range(HOPS):
        chain_a = around(chain_a, 1)
        chain_b = around(chain_b, 1)
        got_a.append(chain_a)
        got_b.append(chain_b)
    got_a[-1] = jnp.where(core == 0, got_a[-1], chip_a)
    got_b[-1] = jnp.where(core == 0, got_b[-1], chip_b)
    keep, send, pa, pb = experts(
        jnp.stack([z * NX, core]),
        jnp.concatenate(got_a, axis=0),
        jnp.concatenate(got_b, axis=0),
        wa.reshape(NDP, NX, feat // NDP, 3 * hid),
    )
    grads = add(keep, swap(send))
    summed = lax.psum_scatter(
        grads.reshape(-1, 3 * hid), ("y", "x"), scatter_dimension=0, tiled=True
    )

    def block(part, hop):
        return part[(hop - 1) * pair_rows : hop * pair_rows]

    none = jnp.zeros((), BF)
    chain_a = jnp.where(core == 0, block(pa, HOPS), none)
    chain_b = jnp.where(core == 0, block(pb, HOPS), none)
    for hop in range(HOPS, 0, -1):
        chain_a = around(chain_a, -1)
        chain_b = around(chain_b, -1)
        if hop > 1:
            chain_a = add(chain_a, block(pa, hop - 1))
            chain_b = add(chain_b, block(pb, hop - 1))
    chain_a = add(chain_a, jnp.where(core == 0, none, block(pa, HOPS)))
    chain_b = add(chain_b, jnp.where(core == 0, none, block(pb, HOPS)))
    total_a = chain_a[:rows].astype(F32) + swap(chain_a[rows:]).astype(F32)
    total_b = chain_b[:rows].astype(F32) + swap(chain_b[rows:]).astype(F32)
    layer_out = total_a[:, :feat].astype(BF)
    token_grad = total_b.astype(BF)
    pair = total_a[:, feat : feat + half] + total_a[:, feat + half :]
    route_grad = jnp.sum(jnp.where(hot, pair[:, None, :], 0.0), 2)
    return (layer_out, token_grad, route_grad, *unpack(summed))


def solution(mesh):
    grid = Mesh(mesh.devices.reshape(NY, NC, NX, NZ), ("y", "c", "x", "z"))
    dp, ex = ("y", "c"), ("x", "z")
    rowwise = P(dp + ex, None)
    weights = (P(ex, dp, None), P(ex, dp, None), P(ex, None, dp))
    return jax.shard_map(
        shards,
        mesh=grid,
        in_specs=(rowwise, rowwise, rowwise, rowwise, *weights),
        out_specs=(rowwise, rowwise, rowwise, *weights),
        check_vma=False,
    )
```

```python
import jax
import jax.numpy as jnp
from jax import lax
from jax.experimental import pallas as pl
from jax.experimental.pallas import tpu as pltpu
from jax.sharding import Mesh
from jax.sharding import PartitionSpec as P

BF = jnp.bfloat16
F32 = jnp.float32
NX, NY, NZ, NC = 4, 4, 16, 2
NDP = NY * NC
HOPS = NZ // 2
ROOM = 32
AUX = 128
PLANES = 8
BLOCK = 128


def dot(a, b, ca, cb):
    return lax.dot_general(a, b, (((ca,), (cb,)), ((), ())), preferred_element_type=F32)


def flat(v):
    return v.reshape(v.shape[0] * v.shape[1], v.shape[2])


def moe_kernel(
    ids_ref, xa_ref, xb_ref, wt_ref, xe_ref, de_ref, act_ref, wh_ref, pa_ref, pb_ref, pos_s, w_s, sel_s, rows_s
):
    e = pl.program_id(0)
    col = ids_ref[0]
    feat = xb_ref.shape[1]
    hid = wt_ref.shape[3] // 3
    spans = [slice(b * BLOCK, (b + 1) * BLOCK) for b in range(HOPS)]
    slot = lax.broadcasted_iota(jnp.int32, (ROOM, BLOCK), 0)

    @pl.when(e == 0)
    def _():
        row = lax.broadcasted_iota(jnp.int32, (PLANES, AUX), 0)
        lane = lax.broadcasted_iota(jnp.int32, (PLANES, AUX), 1)
        want = (row < NX) & ((lane == col + row) | (lane == col + row + AUX // 2))
        w = dot(jnp.where(want, 1.0, 0.0).astype(BF), xa_ref[:, feat:], 1, 1)
        w_s[...] = w
        live = jnp.where(w > 0.0, 1.0, 0.0)
        r = lax.broadcasted_iota(jnp.int32, (BLOCK, BLOCK), 0)
        c = lax.broadcasted_iota(jnp.int32, (BLOCK, BLOCK), 1)
        upper = jnp.where(r <= c, 1.0, 0.0).astype(BF)
        for b, span in enumerate(spans):
            part = live[:, span]
            rank = dot(part.astype(BF), upper, 1, 0) - 1.0
            pos = jnp.where(part > 0.0, rank, -1.0).astype(jnp.int32)
            pos_s[:, span] = pos
            sel = jnp.concatenate(
                [jnp.where(pos[j : j + 1] == slot, 1.0, 0.0) for j in range(NX)], axis=0
            ).astype(BF)
            sel_s[b] = sel
            xe_ref[b] = dot(sel, xa_ref[span, :feat], 1, 0).astype(BF).reshape(NX, ROOM, feat)
            de_ref[b] = dot(sel, xb_ref[span, :], 1, 0).astype(BF).reshape(NX, ROOM, feat)

    xe = flat(xe_ref[:, e])
    de = flat(de_ref[:, e])
    pos = pos_s[pl.ds(e, 1), :]
    wrow = w_s[pl.ds(e, 1), :]
    w = jnp.concatenate(
        [
            jnp.sum(jnp.where(pos[:, span] == slot, wrow[:, span], 0.0), axis=1, keepdims=True)
            for span in spans
        ],
        axis=0,
    )
    wt = wt_ref[:, 0].reshape(feat, 3 * hid)
    gu = dot(xe, wt[:, : 2 * hid], 1, 0)
    hd = dot(de, wt[:, 2 * hid :], 1, 0)
    g = gu[:, :hid]
    u = gu[:, hid:]
    s = jax.nn.sigmoid(g)
    gs = g * s
    h = gs * u
    rg = jnp.sum(h * hd, axis=1, keepdims=True)
    wh = (w * h).astype(BF)
    hg = w * hd
    gb = (hg * u * s * (1.0 + g * (1.0 - s))).astype(BF)
    ub = (hg * gs).astype(BF)
    act = jnp.concatenate([gb, ub], axis=1)
    act_ref[:, e] = act.reshape(HOPS, ROOM, 2 * hid)
    wh_ref[:, e] = wh.reshape(HOPS, ROOM, hid)
    y = dot(wh, wt[:, 2 * hid :], 1, 1).astype(BF)
    rows_s[:, e, :, :feat] = y.reshape(HOPS, ROOM, feat)
    lane = lax.broadcasted_iota(jnp.int32, (HOPS * ROOM, AUX), 1)
    mine = col + e
    rg_hi = rg.astype(BF).astype(F32)
    aux = jnp.where(lane == mine, rg_hi, 0.0) + jnp.where(lane == mine + AUX // 2, rg - rg_hi, 0.0)
    rows_s[:, e, :, feat : feat + AUX] = aux.astype(BF).reshape(HOPS, ROOM, AUX)
    dx = dot(act, wt[:, : 2 * hid], 1, 1).astype(BF)
    rows_s[:, e, :, feat + AUX :] = dx.reshape(HOPS, ROOM, feat)

    @pl.when(e == NX - 1)
    def _():
        for b, span in enumerate(spans):
            rows = flat(rows_s[b])
            pa_ref[span, :] = dot(sel_s[b], rows[:, : feat + AUX], 0, 0).astype(BF)
            pb_ref[span, :] = dot(sel_s[b], rows[:, feat + AUX :], 0, 0).astype(BF)


def experts(ids, xa, xb, wt):
    tok, feat = xb.shape
    hid3 = wt.shape[3]
    hid = hid3 // 3
    rows = feat // NDP
    width = 2 * feat + AUX
    slots = HOPS * NX * ROOM
    flops = 2 * slots * (BLOCK * width * 2 + 6 * feat * hid)
    whole2 = lambda e, s: (0, 0)
    whole4 = lambda e, s: (0, 0, 0, 0)
    packed = lambda n: (HOPS, NX, ROOM, n)
    return pl.pallas_call(
        moe_kernel,
        grid_spec=pltpu.PrefetchScalarGridSpec(
            num_scalar_prefetch=1,
            grid=(NX,),
            in_specs=[
                pl.BlockSpec((tok, feat + AUX), whole2),
                pl.BlockSpec((tok, feat), whole2),
                pl.BlockSpec((NDP, 1, rows, hid3), lambda e, s: (0, e, 0, 0)),
            ],
            out_specs=[
                pl.BlockSpec(packed(feat), whole4),
                pl.BlockSpec(packed(feat), whole4),
                pl.BlockSpec(packed(2 * hid), whole4),
                pl.BlockSpec(packed(hid), whole4),
                pl.BlockSpec((tok, feat + AUX), whole2),
                pl.BlockSpec((tok, feat), whole2),
            ],
            scratch_shapes=[
                pltpu.VMEM((PLANES, tok), jnp.int32),
                pltpu.VMEM((PLANES, tok), F32),
                pltpu.VMEM((HOPS, NX * ROOM, BLOCK), BF),
                pltpu.VMEM(packed(width), BF),
            ],
        ),
        out_shape=[
            jax.ShapeDtypeStruct(packed(feat), BF),
            jax.ShapeDtypeStruct(packed(feat), BF),
            jax.ShapeDtypeStruct(packed(2 * hid), BF),
            jax.ShapeDtypeStruct(packed(hid), BF),
            jax.ShapeDtypeStruct((tok, feat + AUX), BF),
            jax.ShapeDtypeStruct((tok, feat), BF),
        ],
        cost_estimate=pl.CostEstimate(
            flops=flops, bytes_accessed=26_000_000, transcendentals=slots * hid
        ),
    )(ids, xa, xb, wt)


def grad_kernel(ids_ref, xe_ref, de_ref, act_ref, wh_ref, gu_ref, keep_ref, send_ref):
    core = ids_ref[1]
    xe = flat(xe_ref[:, 0])
    de = flat(de_ref[:, 0])
    act = flat(act_ref[:, 0])
    wh = flat(wh_ref[:, 0])
    step = gu_ref.shape[2]
    gu_ref[:, 0] = dot(xe, act, 0, 0).astype(BF).reshape(NDP, step, act.shape[1])
    even = jnp.concatenate([de[:, i * step : (i + 1) * step] for i in range(0, NDP, 2)], axis=1)
    odd = jnp.concatenate([de[:, i * step : (i + 1) * step] for i in range(1, NDP, 2)], axis=1)
    keep = dot(jnp.where(core == 0, even, odd), wh, 0, 0)
    send = dot(jnp.where(core == 0, odd, even), wh, 0, 0)
    keep_ref[:, 0] = keep.astype(BF).reshape(NY, step, wh.shape[1])
    send_ref[:, 0] = send.astype(BF).reshape(NY, step, wh.shape[1])


def weight_grads(ids, xe, de, act, wh):
    feat, hid = xe.shape[3], wh.shape[3]
    rows = feat // NDP
    one = lambda n: pl.BlockSpec((HOPS, 1, ROOM, n), lambda e, s: (0, e, 0, 0))
    out = lambda n, w: pl.BlockSpec((n, 1, rows, w), lambda e, s: (0, e, 0, 0))
    return pl.pallas_call(
        grad_kernel,
        grid_spec=pltpu.PrefetchScalarGridSpec(
            num_scalar_prefetch=1,
            grid=(NX,),
            in_specs=[one(feat), one(feat), one(2 * hid), one(hid)],
            out_specs=[out(NDP, 2 * hid), out(NY, hid), out(NY, hid)],
        ),
        out_shape=[
            jax.ShapeDtypeStruct((NDP, NX, rows, 2 * hid), BF),
            jax.ShapeDtypeStruct((NY, NX, rows, hid), BF),
            jax.ShapeDtypeStruct((NY, NX, rows, hid), BF),
        ],
        cost_estimate=pl.CostEstimate(
            flops=6 * HOPS * NX * ROOM * feat * hid, bytes_accessed=16_000_000, transcendentals=0
        ),
    )(ids, xe, de, act, wh)


def pack_kernel(g_ref, u_ref, d_ref, o_ref):
    hid = g_ref.shape[2]
    o_ref[:, :hid] = g_ref[0]
    o_ref[:, hid : 2 * hid] = u_ref[0]
    o_ref[:, 2 * hid :] = d_ref[0].astype(F32).T.astype(BF)


def pack(g, u, d):
    return pl.pallas_call(
        pack_kernel, out_shape=jax.ShapeDtypeStruct((g.shape[1], 3 * g.shape[2]), BF)
    )(g, u, d)


def unpack_kernel(s_ref, d_ref, g_out, u_out, d_out):
    hid = g_out.shape[2]
    g_out[0] = s_ref[:, :hid].astype(F32)
    u_out[0] = s_ref[:, hid:].astype(F32)
    d = d_ref[0].astype(F32)
    for i in range(1, NX):
        d = d + d_ref[i].astype(F32)
    d_out[0] = d.T


def unpack(s, d):
    rows, hid = s.shape[0], s.shape[1] // 2
    return pl.pallas_call(
        unpack_kernel,
        out_shape=[
            jax.ShapeDtypeStruct((1, rows, hid), F32),
            jax.ShapeDtypeStruct((1, rows, hid), F32),
            jax.ShapeDtypeStruct((1, hid, rows), F32),
        ],
    )(s, d)


def around(value, sign):
    pairs = [(z, (z + sign) % NZ) for z in range(NZ)]
    pairs += [(NZ + z, NZ + (z - sign) % NZ) for z in range(NZ)]
    return lax.ppermute(value, ("c", "z"), pairs)


def swap(value):
    return lax.ppermute(value, "c", [(0, 1), (1, 0)])


def add(a, b):
    return (a.astype(F32) + b.astype(F32)).astype(BF)


def shards(tokens, expert_ids, route_weight, out_grad, gate_weight, up_weight, down_weight):
    rows, feat = tokens.shape
    hid = gate_weight.shape[2]
    z = lax.axis_index("z").astype(jnp.int32)
    core = lax.axis_index("c").astype(jnp.int32)
    half = AUX // 2
    pair_rows = 2 * rows
    wa = lax.all_gather(pack(gate_weight, up_weight, down_weight), ("y", "c", "x"), axis=0, tiled=True)
    place = (expert_ids % NZ) * NX + expert_ids // NZ
    hot = place[:, :, None] == jnp.arange(half, dtype=jnp.int32)
    dense = jnp.sum(jnp.where(hot, route_weight[:, :, None], 0.0), 1)
    hi = lax.reduce_precision(dense, 8, 7)
    own_a = jnp.concatenate([tokens, hi.astype(BF), (dense - hi).astype(BF)], axis=1)
    chain_a = chip_a = jnp.concatenate([own_a, swap(own_a)], axis=0)
    chain_b = chip_b = jnp.concatenate([out_grad, swap(out_grad)], axis=0)
    got_a, got_b = [], []
    for _ in range(HOPS):
        chain_a = around(chain_a, 1)
        chain_b = around(chain_b, 1)
        got_a.append(chain_a)
        got_b.append(chain_b)
    got_a[-1] = jnp.where(core == 0, got_a[-1], chip_a)
    got_b[-1] = jnp.where(core == 0, got_b[-1], chip_b)
    ids = jnp.stack([z * NX, core])
    *saved, pa, pb = experts(
        ids,
        jnp.concatenate(got_a, axis=0),
        jnp.concatenate(got_b, axis=0),
        wa.reshape(NDP, NX, feat // NDP, 3 * hid),
    )
    gu, keep, send = weight_grads(ids, *saved)
    summed = lax.psum_scatter(
        gu.reshape(-1, 2 * hid), ("y", "c", "x"), scatter_dimension=0, tiled=True
    )
    down = swap(send)
    down = add(keep, down)
    down = lax.all_to_all(down, "y", 0, 0, tiled=True)
    down = jnp.sum(down.astype(F32), 0).astype(BF)
    down = lax.all_to_all(down, "x", 0, 0, tiled=True)

    def block(part, hop):
        return part[(hop - 1) * pair_rows : hop * pair_rows]

    none = jnp.zeros((), BF)
    chain_a = jnp.where(core == 0, block(pa, HOPS), none)
    chain_b = jnp.where(core == 0, block(pb, HOPS), none)
    for hop in range(HOPS, 0, -1):
        chain_a = around(chain_a, -1)
        chain_b = around(chain_b, -1)
        if hop > 1:
            chain_a = add(chain_a, block(pa, hop - 1))
            chain_b = add(chain_b, block(pb, hop - 1))
    chain_a = add(chain_a, jnp.where(core == 0, none, block(pa, HOPS)))
    chain_b = add(chain_b, jnp.where(core == 0, none, block(pb, HOPS)))
    total_a = chain_a[:rows].astype(F32) + swap(chain_a[rows:]).astype(F32)
    total_b = chain_b[:rows].astype(F32) + swap(chain_b[rows:]).astype(F32)
    layer_out = total_a[:, :feat].astype(BF)
    token_grad = total_b.astype(BF)
    pair = total_a[:, feat : feat + half] + total_a[:, feat + half :]
    route_grad = jnp.sum(jnp.where(hot, pair[:, None, :], 0.0), 2)
    return (layer_out, token_grad, route_grad, *unpack(summed, down))


def solution(mesh):
    grid = Mesh(mesh.devices.reshape(NY, NC, NX, NZ), ("y", "c", "x", "z"))
    dp, ex = ("y", "c"), ("x", "z")
    rowwise = P(dp + ex, None)
    weights = (P(ex, dp, None), P(ex, dp, None), P(ex, None, dp))
    return jax.shard_map(
        shards,
        mesh=grid,
        in_specs=(rowwise, rowwise, rowwise, rowwise, *weights),
        out_specs=(rowwise, rowwise, rowwise, *weights),
        check_vma=False,
    )
```

```python
import jax
import jax.numpy as jnp
from jax import lax
from jax.experimental import pallas as pl
from jax.experimental.pallas import tpu as pltpu
from jax.sharding import Mesh
from jax.sharding import PartitionSpec as P

BF = jnp.bfloat16
F32 = jnp.float32
NX, NY, NZ, NC = 4, 4, 16, 2
NDP = NY * NC
HOPS = NZ // 2
CAP = 10
SLOTS = NZ * CAP
AUX = 128
PLANES = 8


def dot(a, b, ca, cb):
    return lax.dot_general(a, b, (((ca,), (cb,)), ((), ())), preferred_element_type=F32)


def grad_kernel(
    ids_ref, xa_ref, xb_ref, wt_ref, keep_ref, send_ref, act_ref, wh_ref, aux_ref, sel_ref, w_s, pos_s, xe_s, de_s
):
    e = pl.program_id(0)
    col = ids_ref[0]
    core = ids_ref[1]
    tok = xa_ref.shape[0]
    feat = xb_ref.shape[1]
    hid = wt_ref.shape[3] // 3
    slot = lax.broadcasted_iota(jnp.int32, (SLOTS, tok), 0)

    @pl.when(e == 0)
    def _():
        row = lax.broadcasted_iota(jnp.int32, (PLANES, AUX), 0)
        lane = lax.broadcasted_iota(jnp.int32, (PLANES, AUX), 1)
        want = (row < NX) & ((lane == col + row) | (lane == col + row + AUX // 2))
        w = dot(jnp.where(want, 1.0, 0.0).astype(BF), xa_ref[:, feat:], 1, 1)
        w_s[...] = w
        live = jnp.where(w > 0.0, 1.0, 0.0)
        r = lax.broadcasted_iota(jnp.int32, (128, 128), 0)
        c = lax.broadcasted_iota(jnp.int32, (128, 128), 1)
        upper = jnp.where(r <= c, 1.0, 0.0).astype(BF)
        before = jnp.full((PLANES, 1), -1.0, F32)
        for lo in range(0, tok, 128):
            part = live[:, lo : lo + 128]
            rank = dot(part.astype(BF), upper, 1, 0) + before
            pos_s[:, lo : lo + 128] = jnp.where(part > 0.0, rank, -1.0).astype(jnp.int32)
            before = before + jnp.sum(part, axis=1, keepdims=True)
        for j in range(NX):
            hit = pos_s[j : j + 1, :] == slot
            sel_ref[j * SLOTS : (j + 1) * SLOTS, :] = jnp.where(hit, 1.0, 0.0).astype(BF)
        for lo in range(0, feat, 512):
            span = slice(lo, lo + 512)
            xe_s[:, span] = dot(sel_ref[...], xa_ref[:, span], 1, 0).astype(BF)
            de_s[:, span] = dot(sel_ref[...], xb_ref[:, span], 1, 0).astype(BF)

    here = pl.ds(pl.multiple_of(e * SLOTS, SLOTS), SLOTS)
    xe = xe_s[here, :]
    de = de_s[here, :]
    picked = pos_s[pl.ds(e, 1), :] == slot
    w = jnp.sum(jnp.where(picked, w_s[pl.ds(e, 1), :], 0.0), axis=1, keepdims=True)
    wt = wt_ref[:, 0].reshape(feat, 3 * hid)
    gu = dot(xe, wt[:, : 2 * hid], 1, 0)
    hd = dot(de, wt[:, 2 * hid :], 1, 0)
    g = gu[:, :hid]
    u = gu[:, hid:]
    s = jax.nn.sigmoid(g)
    gs = g * s
    h = gs * u
    rg = jnp.sum(h * hd, axis=1, keepdims=True)
    wh = (w * h).astype(BF)
    hg = w * hd
    gb = (hg * u * s * (1.0 + g * (1.0 - s))).astype(BF)
    ub = (hg * gs).astype(BF)
    act = jnp.concatenate([gb, ub], axis=1)
    act_ref[...] = act
    wh_ref[...] = wh
    lane = lax.broadcasted_iota(jnp.int32, (SLOTS, AUX), 1)
    mine = col + e
    rg_hi = rg.astype(BF).astype(F32)
    aux = jnp.where(lane == mine, rg_hi, 0.0) + jnp.where(lane == mine + AUX // 2, rg - rg_hi, 0.0)
    aux_ref[...] = aux.astype(BF)
    step = feat // NDP

    def halves(v):
        even = jnp.concatenate([v[:, i * step : (i + 1) * step] for i in range(0, NDP, 2)], axis=1)
        odd = jnp.concatenate([v[:, i * step : (i + 1) * step] for i in range(1, NDP, 2)], axis=1)
        return jnp.where(core == 0, even, odd), jnp.where(core == 0, odd, even)

    xk, xs = halves(xe)
    dk, ds = halves(de)
    keep_ref[:, 0, :, : 2 * hid] = dot(xk, act, 0, 0).astype(BF).reshape(NY, step, 2 * hid)
    keep_ref[:, 0, :, 2 * hid :] = dot(dk, wh, 0, 0).astype(BF).reshape(NY, step, hid)
    send_ref[:, 0, :, : 2 * hid] = dot(xs, act, 0, 0).astype(BF).reshape(NY, step, 2 * hid)
    send_ref[:, 0, :, 2 * hid :] = dot(ds, wh, 0, 0).astype(BF).reshape(NY, step, hid)


def expert_grads(ids, xa, xb, wt):
    tok, feat = xb.shape
    hid3 = wt.shape[3]
    hid = hid3 // 3
    rows = feat // NDP
    slots = NX * SLOTS
    whole = lambda e, s: (0, 0)
    expert = lambda e, s: (0, e, 0, 0)
    slotted = lambda e, s: (e, 0)
    return pl.pallas_call(
        grad_kernel,
        grid_spec=pltpu.PrefetchScalarGridSpec(
            num_scalar_prefetch=1,
            grid=(NX,),
            in_specs=[
                pl.BlockSpec((tok, feat + AUX), whole),
                pl.BlockSpec((tok, feat), whole),
                pl.BlockSpec((NDP, 1, rows, hid3), expert),
            ],
            out_specs=[
                pl.BlockSpec((NY, 1, rows, hid3), expert),
                pl.BlockSpec((NY, 1, rows, hid3), expert),
                pl.BlockSpec((SLOTS, 2 * hid), slotted),
                pl.BlockSpec((SLOTS, hid), slotted),
                pl.BlockSpec((SLOTS, AUX), slotted),
                pl.BlockSpec((slots, tok), whole),
            ],
            scratch_shapes=[
                pltpu.VMEM((PLANES, tok), F32),
                pltpu.VMEM((PLANES, tok), jnp.int32),
                pltpu.VMEM((slots, feat), BF),
                pltpu.VMEM((slots, feat), BF),
            ],
        ),
        out_shape=[
            jax.ShapeDtypeStruct((NY, NX, rows, hid3), BF),
            jax.ShapeDtypeStruct((NY, NX, rows, hid3), BF),
            jax.ShapeDtypeStruct((slots, 2 * hid), BF),
            jax.ShapeDtypeStruct((slots, hid), BF),
            jax.ShapeDtypeStruct((slots, AUX), BF),
            jax.ShapeDtypeStruct((slots, tok), BF),
        ],
        cost_estimate=pl.CostEstimate(
            flops=2 * slots * feat * (2 * tok + 6 * hid),
            bytes_accessed=26_000_000,
            transcendentals=slots * hid,
        ),
    )(ids, xa, xb, wt)


def merge_kernel(act_ref, wh_ref, aux_ref, sel_ref, wt_ref, pa_ref, pb_ref, rows_s):
    e = pl.program_id(0)
    feat = pb_ref.shape[1]
    hid = wh_ref.shape[1]
    here = pl.ds(pl.multiple_of(e * SLOTS, SLOTS), SLOTS)
    wt = wt_ref[:, 0].reshape(feat, 3 * hid)
    rows_s[here, :feat] = dot(wh_ref[...], wt[:, 2 * hid :], 1, 1).astype(BF)
    rows_s[here, feat : feat + AUX] = aux_ref[...]
    rows_s[here, feat + AUX :] = dot(act_ref[...], wt[:, : 2 * hid], 1, 1).astype(BF)

    @pl.when(e == NX - 1)
    def _():
        for lo in range(0, feat + AUX, 384):
            pa_ref[:, lo : lo + 384] = dot(sel_ref[...], rows_s[:, lo : lo + 384], 0, 0).astype(BF)
        for lo in range(0, feat, 512):
            off = feat + AUX + lo
            pb_ref[:, lo : lo + 512] = dot(sel_ref[...], rows_s[:, off : off + 512], 0, 0).astype(BF)


def merge(act, wh, aux, sel, wt):
    slots, tok = sel.shape
    hid = wh.shape[1]
    rows = wt.shape[2]
    feat = rows * NDP
    whole = lambda e: (0, 0)
    slotted = lambda e: (e, 0)
    return pl.pallas_call(
        merge_kernel,
        grid=(NX,),
        in_specs=[
            pl.BlockSpec((SLOTS, 2 * hid), slotted),
            pl.BlockSpec((SLOTS, hid), slotted),
            pl.BlockSpec((SLOTS, AUX), slotted),
            pl.BlockSpec((slots, tok), whole),
            pl.BlockSpec((NDP, 1, rows, 3 * hid), lambda e: (0, e, 0, 0)),
        ],
        out_specs=[
            pl.BlockSpec((tok, feat + AUX), whole),
            pl.BlockSpec((tok, feat), whole),
        ],
        scratch_shapes=[pltpu.VMEM((slots, 2 * feat + AUX), BF)],
        out_shape=[
            jax.ShapeDtypeStruct((tok, feat + AUX), BF),
            jax.ShapeDtypeStruct((tok, feat), BF),
        ],
        cost_estimate=pl.CostEstimate(
            flops=2 * slots * feat * (2 * tok + 3 * hid), bytes_accessed=16_000_000, transcendentals=0
        ),
    )(act, wh, aux, sel, wt)


def pack_kernel(g_ref, u_ref, d_ref, o_ref):
    hid = g_ref.shape[2]
    o_ref[:, :hid] = g_ref[0]
    o_ref[:, hid : 2 * hid] = u_ref[0]
    o_ref[:, 2 * hid :] = d_ref[0].astype(F32).T.astype(BF)


def pack(g, u, d):
    return pl.pallas_call(
        pack_kernel, out_shape=jax.ShapeDtypeStruct((g.shape[1], 3 * g.shape[2]), BF)
    )(g, u, d)


def unpack_kernel(s_ref, g_ref, u_ref, d_ref):
    hid = g_ref.shape[2]
    g_ref[0] = s_ref[:, :hid].astype(F32)
    u_ref[0] = s_ref[:, hid : 2 * hid].astype(F32)
    d_ref[0] = s_ref[:, 2 * hid :].astype(F32).T


def unpack(s):
    rows, hid = s.shape[0], s.shape[1] // 3
    return pl.pallas_call(
        unpack_kernel,
        out_shape=[
            jax.ShapeDtypeStruct((1, rows, hid), F32),
            jax.ShapeDtypeStruct((1, rows, hid), F32),
            jax.ShapeDtypeStruct((1, hid, rows), F32),
        ],
    )(s)


def around(value, sign):
    pairs = [(z, (z + sign) % NZ) for z in range(NZ)]
    pairs += [(NZ + z, NZ + (z - sign) % NZ) for z in range(NZ)]
    return lax.ppermute(value, ("c", "z"), pairs)


def swap(value):
    return lax.ppermute(value, "c", [(0, 1), (1, 0)])


def add(a, b):
    return (a.astype(F32) + b.astype(F32)).astype(BF)


def shards(tokens, expert_ids, route_weight, out_grad, gate_weight, up_weight, down_weight):
    rows, feat = tokens.shape
    hid = gate_weight.shape[2]
    z = lax.axis_index("z").astype(jnp.int32)
    core = lax.axis_index("c").astype(jnp.int32)
    half = AUX // 2
    pair_rows = 2 * rows
    wa = lax.all_gather(pack(gate_weight, up_weight, down_weight), ("y", "c", "x"), axis=0, tiled=True)
    place = (expert_ids % NZ) * NX + expert_ids // NZ
    hot = place[:, :, None] == jnp.arange(half, dtype=jnp.int32)
    dense = jnp.sum(jnp.where(hot, route_weight[:, :, None], 0.0), 1)
    hi = lax.reduce_precision(dense, 8, 7)
    own_a = jnp.concatenate([tokens, hi.astype(BF), (dense - hi).astype(BF)], axis=1)
    chain_a = chip_a = jnp.concatenate([own_a, swap(own_a)], axis=0)
    chain_b = chip_b = jnp.concatenate([out_grad, swap(out_grad)], axis=0)
    got_a, got_b = [], []
    for _ in range(HOPS):
        chain_a = around(chain_a, 1)
        chain_b = around(chain_b, 1)
        got_a.append(chain_a)
        got_b.append(chain_b)
    got_a[-1] = jnp.where(core == 0, got_a[-1], chip_a)
    got_b[-1] = jnp.where(core == 0, got_b[-1], chip_b)
    wt = wa.reshape(NDP, NX, feat // NDP, 3 * hid)
    keep, send, *saved = expert_grads(
        jnp.stack([z * NX, core]), jnp.concatenate(got_a, axis=0), jnp.concatenate(got_b, axis=0), wt
    )
    send = swap(send)
    pa, pb = merge(*saved, wt)
    summed = lax.psum_scatter(
        add(keep, send).reshape(-1, 3 * hid), ("y", "x"), scatter_dimension=0, tiled=True
    )

    def block(part, hop):
        return part[(hop - 1) * pair_rows : hop * pair_rows]

    none = jnp.zeros((), BF)
    chain_a = jnp.where(core == 0, block(pa, HOPS), none)
    chain_b = jnp.where(core == 0, block(pb, HOPS), none)
    for hop in range(HOPS, 0, -1):
        chain_a = around(chain_a, -1)
        chain_b = around(chain_b, -1)
        if hop > 1:
            chain_a = add(chain_a, block(pa, hop - 1))
            chain_b = add(chain_b, block(pb, hop - 1))
    chain_a = add(chain_a, jnp.where(core == 0, none, block(pa, HOPS)))
    chain_b = add(chain_b, jnp.where(core == 0, none, block(pb, HOPS)))
    total_a = chain_a[:rows].astype(F32) + swap(chain_a[rows:]).astype(F32)
    total_b = chain_b[:rows].astype(F32) + swap(chain_b[rows:]).astype(F32)
    layer_out = total_a[:, :feat].astype(BF)
    token_grad = total_b.astype(BF)
    pair = total_a[:, feat : feat + half] + total_a[:, feat + half :]
    route_grad = jnp.sum(jnp.where(hot, pair[:, None, :], 0.0), 2)
    return (layer_out, token_grad, route_grad, *unpack(summed))


def solution(mesh):
    grid = Mesh(mesh.devices.reshape(NY, NC, NX, NZ), ("y", "c", "x", "z"))
    dp, ex = ("y", "c"), ("x", "z")
    rowwise = P(dp + ex, None)
    weights = (P(ex, dp, None), P(ex, dp, None), P(ex, None, dp))
    return jax.shard_map(
        shards,
        mesh=grid,
        in_specs=(rowwise, rowwise, rowwise, rowwise, *weights),
        out_specs=(rowwise, rowwise, rowwise, *weights),
        check_vma=False,
    )
```

```python
import jax
import jax.numpy as jnp
from jax import lax
from jax.experimental import pallas as pl
from jax.experimental.pallas import tpu as pltpu
from jax.sharding import Mesh
from jax.sharding import PartitionSpec as P

BF = jnp.bfloat16
F32 = jnp.float32
NX, NY, NZ, NC = 4, 4, 16, 2
NDP = NY * NC
HOPS = NZ // 2
CAP = 10
SLOTS = NZ * CAP
AUX = 128
PLANES = 8
MERGE = 256


def dot(a, b, ca, cb):
    return lax.dot_general(a, b, (((ca,), (cb,)), ((), ())), preferred_element_type=F32)


def moe_kernel(ids_ref, xa_ref, xb_ref, wt_ref, keep_ref, send_ref, pa_ref, pb_ref, pos_s, post_s, w_s, sel_s, xe_s, de_s, rows_s):
    e = pl.program_id(0)
    col = ids_ref[0]
    core = ids_ref[1]
    tok = xa_ref.shape[0]
    feat = xb_ref.shape[1]
    hid = wt_ref.shape[3] // 3
    slots = NX * SLOTS
    slot = lax.broadcasted_iota(jnp.int32, (SLOTS, tok), 0)

    @pl.when(e == 0)
    def _():
        row = lax.broadcasted_iota(jnp.int32, (PLANES, AUX), 0)
        lane = lax.broadcasted_iota(jnp.int32, (PLANES, AUX), 1)
        want = (row < NX) & ((lane == col + row) | (lane == col + row + AUX // 2))
        w = dot(jnp.where(want, 1.0, 0.0).astype(BF), xa_ref[:, feat:], 1, 1)
        w_s[...] = w
        live = jnp.where(w > 0.0, 1.0, 0.0)
        r = lax.broadcasted_iota(jnp.int32, (128, 128), 0)
        c = lax.broadcasted_iota(jnp.int32, (128, 128), 1)
        upper = jnp.where(r <= c, 1.0, 0.0).astype(BF)
        before = jnp.full((PLANES, 1), -1.0, F32)
        for lo in range(0, tok, 128):
            part = live[:, lo : lo + 128]
            rank = dot(part.astype(BF), upper, 1, 0) + before
            pos = jnp.where(part > 0.0, rank, -float(slots))
            pos_s[:, lo : lo + 128] = pos.astype(jnp.int32)
            post_s[lo : lo + 128, :] = pos.T
            before = before + jnp.sum(part, axis=1, keepdims=True)
        for j in range(NX):
            hit = pos_s[j : j + 1, :] == slot
            sel_s[j * SLOTS : (j + 1) * SLOTS, :] = jnp.where(hit, 1.0, 0.0).astype(BF)
        for lo in range(0, feat, 512):
            span = slice(lo, lo + 512)
            xe_s[:, span] = dot(sel_s[...], xa_ref[:, span], 1, 0).astype(BF)
            de_s[:, span] = dot(sel_s[...], xb_ref[:, span], 1, 0).astype(BF)

    here = pl.ds(pl.multiple_of(e * SLOTS, SLOTS), SLOTS)
    xe = xe_s[here, :]
    de = de_s[here, :]
    picked = pos_s[pl.ds(e, 1), :] == slot
    w = jnp.sum(jnp.where(picked, w_s[pl.ds(e, 1), :], 0.0), axis=1, keepdims=True)
    wt = wt_ref[:, 0].reshape(feat, 3 * hid)
    gu = dot(xe, wt[:, : 2 * hid], 1, 0)
    hd = dot(de, wt[:, 2 * hid :], 1, 0)
    g = gu[:, :hid]
    u = gu[:, hid:]
    s = jax.nn.sigmoid(g)
    gs = g * s
    h = gs * u
    rg = jnp.sum(h * hd, axis=1, keepdims=True)
    wh = (w * h).astype(BF)
    hg = w * hd
    gb = (hg * u * s * (1.0 + g * (1.0 - s))).astype(BF)
    ub = (hg * gs).astype(BF)
    act = jnp.concatenate([gb, ub], axis=1)
    rows_s[here, :feat] = dot(wh, wt[:, 2 * hid :], 1, 1).astype(BF)
    lane = lax.broadcasted_iota(jnp.int32, (SLOTS, AUX), 1)
    mine = col + e
    rg_hi = rg.astype(BF).astype(F32)
    aux = jnp.where(lane == mine, rg_hi, 0.0) + jnp.where(lane == mine + AUX // 2, rg - rg_hi, 0.0)
    rows_s[here, feat : feat + AUX] = aux.astype(BF)
    rows_s[here, feat + AUX :] = dot(act, wt[:, : 2 * hid], 1, 1).astype(BF)
    step = feat // NDP

    def halves(v):
        even = jnp.concatenate([v[:, i * step : (i + 1) * step] for i in range(0, NDP, 2)], axis=1)
        odd = jnp.concatenate([v[:, i * step : (i + 1) * step] for i in range(1, NDP, 2)], axis=1)
        return jnp.where(core == 0, even, odd), jnp.where(core == 0, odd, even)

    xk, xs = halves(xe)
    dk, ds = halves(de)
    keep_ref[:, 0, :, : 2 * hid] = dot(xk, act, 0, 0).astype(BF).reshape(NY, step, 2 * hid)
    keep_ref[:, 0, :, 2 * hid :] = dot(dk, wh, 0, 0).astype(BF).reshape(NY, step, hid)
    send_ref[:, 0, :, : 2 * hid] = dot(xs, act, 0, 0).astype(BF).reshape(NY, step, 2 * hid)
    send_ref[:, 0, :, 2 * hid :] = dot(ds, wh, 0, 0).astype(BF).reshape(NY, step, hid)

    @pl.when(e == NX - 1)
    def _():
        @pl.loop(0, tok // MERGE)
        def _(i):
            span = pl.ds(pl.multiple_of(i * MERGE, MERGE), MERGE)
            lane = lax.broadcasted_iota(jnp.int32, (MERGE, slots), 1).astype(F32)
            sel = jnp.zeros((MERGE, slots), F32)
            for j in range(NX):
                sel = jnp.where(post_s[span, j : j + 1] + float(j * SLOTS) == lane, 1.0, sel)
            sel = sel.astype(BF)
            for lo in range(0, feat + AUX, 384):
                pa_ref[span, lo : lo + 384] = dot(sel, rows_s[:, lo : lo + 384], 1, 0).astype(BF)
            for lo in range(0, feat, 512):
                off = feat + AUX + lo
                pb_ref[span, lo : lo + 512] = dot(sel, rows_s[:, off : off + 512], 1, 0).astype(BF)


def experts(ids, xa, xb, wt):
    tok, feat = xb.shape
    hid3 = wt.shape[3]
    rows = feat // NDP
    slots = NX * SLOTS
    width = 2 * feat + AUX
    flops = 2 * slots * (tok * width * 2 + 9 * feat * hid3 // 3)
    whole = lambda e, s: (0, 0)
    return pl.pallas_call(
        moe_kernel,
        grid_spec=pltpu.PrefetchScalarGridSpec(
            num_scalar_prefetch=1,
            grid=(NX,),
            in_specs=[
                pl.BlockSpec((tok, feat + AUX), whole),
                pl.BlockSpec((tok, feat), whole),
                pl.BlockSpec((NDP, 1, rows, hid3), lambda e, s: (0, e, 0, 0)),
            ],
            out_specs=[
                pl.BlockSpec((NY, 1, rows, hid3), lambda e, s: (0, e, 0, 0)),
                pl.BlockSpec((NY, 1, rows, hid3), lambda e, s: (0, e, 0, 0)),
                pl.BlockSpec((tok, feat + AUX), whole),
                pl.BlockSpec((tok, feat), whole),
            ],
            scratch_shapes=[
                pltpu.VMEM((PLANES, tok), jnp.int32),
                pltpu.VMEM((tok, PLANES), F32),
                pltpu.VMEM((PLANES, tok), F32),
                pltpu.VMEM((slots, tok), BF),
                pltpu.VMEM((slots, feat), BF),
                pltpu.VMEM((slots, feat), BF),
                pltpu.VMEM((slots, width), BF),
            ],
        ),
        out_shape=[
            jax.ShapeDtypeStruct((NY, NX, rows, hid3), BF),
            jax.ShapeDtypeStruct((NY, NX, rows, hid3), BF),
            jax.ShapeDtypeStruct((tok, feat + AUX), BF),
            jax.ShapeDtypeStruct((tok, feat), BF),
        ],
        cost_estimate=pl.CostEstimate(
            flops=flops, bytes_accessed=30_000_000, transcendentals=slots * hid3 // 3
        ),
    )(ids, xa, xb, wt)


def pack_kernel(g_ref, u_ref, d_ref, o_ref):
    hid = g_ref.shape[2]
    o_ref[:, :hid] = g_ref[0]
    o_ref[:, hid : 2 * hid] = u_ref[0]
    o_ref[:, 2 * hid :] = d_ref[0].astype(F32).T.astype(BF)


def pack(g, u, d):
    return pl.pallas_call(
        pack_kernel, out_shape=jax.ShapeDtypeStruct((g.shape[1], 3 * g.shape[2]), BF)
    )(g, u, d)


def unpack_kernel(s_ref, g_ref, u_ref, d_ref):
    hid = g_ref.shape[2]
    g_ref[0] = s_ref[:, :hid].astype(F32)
    u_ref[0] = s_ref[:, hid : 2 * hid].astype(F32)
    d_ref[0] = s_ref[:, 2 * hid :].astype(F32).T


def unpack(s):
    rows, hid = s.shape[0], s.shape[1] // 3
    return pl.pallas_call(
        unpack_kernel,
        out_shape=[
            jax.ShapeDtypeStruct((1, rows, hid), F32),
            jax.ShapeDtypeStruct((1, rows, hid), F32),
            jax.ShapeDtypeStruct((1, hid, rows), F32),
        ],
    )(s)


def around(value, sign, far=False):
    pairs = [(NZ + z, NZ + (z - sign) % NZ) for z in range(NZ)]
    if not far:
        pairs += [(z, (z + sign) % NZ) for z in range(NZ)]
    return lax.ppermute(value, ("c", "z"), pairs)


def swap(value):
    return lax.ppermute(value, "c", [(0, 1), (1, 0)])


def add(a, b):
    return (a.astype(F32) + b.astype(F32)).astype(BF)


def shards(tokens, expert_ids, route_weight, out_grad, gate_weight, up_weight, down_weight):
    rows, feat = tokens.shape
    hid = gate_weight.shape[2]
    z = lax.axis_index("z").astype(jnp.int32)
    core = lax.axis_index("c").astype(jnp.int32)
    half = AUX // 2
    pair_rows = 2 * rows
    wa = lax.all_gather(pack(gate_weight, up_weight, down_weight), ("y", "c", "x"), axis=0, tiled=True)
    place = (expert_ids % NZ) * NX + expert_ids // NZ
    hot = place[:, :, None] == jnp.arange(half, dtype=jnp.int32)
    dense = jnp.sum(jnp.where(hot, route_weight[:, :, None], 0.0), 1)
    hi = lax.reduce_precision(dense, 8, 7)
    own_a = jnp.concatenate([tokens, hi.astype(BF), (dense - hi).astype(BF)], axis=1)
    chain_a = chip_a = jnp.concatenate([own_a, swap(own_a)], axis=0)
    chain_b = chip_b = jnp.concatenate([out_grad, swap(out_grad)], axis=0)
    got_a, got_b = [], []
    for hop in range(1, HOPS + 1):
        chain_a = around(chain_a, 1, hop == HOPS)
        chain_b = around(chain_b, 1, hop == HOPS)
        got_a.append(chain_a)
        got_b.append(chain_b)
    got_a[-1] = jnp.where(core == 0, chip_a, got_a[-1])
    got_b[-1] = jnp.where(core == 0, chip_b, got_b[-1])
    keep, send, pa, pb = experts(
        jnp.stack([z * NX, core]),
        jnp.concatenate(got_a, axis=0),
        jnp.concatenate(got_b, axis=0),
        wa.reshape(NDP, NX, feat // NDP, 3 * hid),
    )
    grads = add(keep, swap(send))
    summed = lax.psum_scatter(
        grads.reshape(-1, 3 * hid), ("y", "x"), scatter_dimension=0, tiled=True
    )

    def block(part, hop):
        return part[(hop - 1) * pair_rows : hop * pair_rows]

    none = jnp.zeros((), BF)
    chain_a = block(pa, HOPS)
    chain_b = block(pb, HOPS)
    for hop in range(HOPS, 0, -1):
        chain_a = around(chain_a, -1, hop == HOPS)
        chain_b = around(chain_b, -1, hop == HOPS)
        if hop > 1:
            chain_a = add(chain_a, block(pa, hop - 1))
            chain_b = add(chain_b, block(pb, hop - 1))
    chain_a = add(chain_a, jnp.where(core == 0, block(pa, HOPS), none))
    chain_b = add(chain_b, jnp.where(core == 0, block(pb, HOPS), none))
    total_a = chain_a[:rows].astype(F32) + swap(chain_a[rows:]).astype(F32)
    total_b = chain_b[:rows].astype(F32) + swap(chain_b[rows:]).astype(F32)
    layer_out = total_a[:, :feat].astype(BF)
    token_grad = total_b.astype(BF)
    pair = total_a[:, feat : feat + half] + total_a[:, feat + half :]
    route_grad = jnp.sum(jnp.where(hot, pair[:, None, :], 0.0), 2)
    return (layer_out, token_grad, route_grad, *unpack(summed))


def solution(mesh):
    grid = Mesh(mesh.devices.reshape(NY, NC, NX, NZ), ("y", "c", "x", "z"))
    dp, ex = ("y", "c"), ("x", "z")
    rowwise = P(dp + ex, None)
    weights = (P(ex, dp, None), P(ex, dp, None), P(ex, None, dp))
    return jax.shard_map(
        shards,
        mesh=grid,
        in_specs=(rowwise, rowwise, rowwise, rowwise, *weights),
        out_specs=(rowwise, rowwise, rowwise, *weights),
        check_vma=False,
    )
```

```python
import jax
import jax.numpy as jnp
from jax import lax
from jax.experimental import pallas as pl
from jax.experimental.pallas import tpu as pltpu
from jax.sharding import Mesh
from jax.sharding import PartitionSpec as P

BF = jnp.bfloat16
F32 = jnp.float32
NX, NY, NZ, NC = 4, 4, 16, 2
NDP = NY * NC
HOPS = NZ // 2
CAP = 10
SLOTS = NZ * CAP
AUX = 128
PLANES = 8
MERGE = 64


def dot(a, b, ca, cb):
    return lax.dot_general(a, b, (((ca,), (cb,)), ((), ())), preferred_element_type=F32)


def moe_kernel(ids_ref, xa_ref, xb_ref, wt_ref, keep_ref, send_ref, pa_ref, pb_ref, pos_s, post_s, w_s, sel_s, selt_s, xe_s, de_s, rows_s):
    e = pl.program_id(0)
    col = ids_ref[0]
    core = ids_ref[1]
    tok = xa_ref.shape[0]
    feat = xb_ref.shape[1]
    hid = wt_ref.shape[3] // 3
    slots = NX * SLOTS
    slot = lax.broadcasted_iota(jnp.int32, (SLOTS, tok), 0)

    @pl.when(e == 0)
    def _():
        row = lax.broadcasted_iota(jnp.int32, (PLANES, AUX), 0)
        lane = lax.broadcasted_iota(jnp.int32, (PLANES, AUX), 1)
        want = (row < NX) & ((lane == col + row) | (lane == col + row + AUX // 2))
        w = dot(jnp.where(want, 1.0, 0.0).astype(BF), xa_ref[:, feat:], 1, 1)
        w_s[...] = w
        live = jnp.where(w > 0.0, 1.0, 0.0)
        r = lax.broadcasted_iota(jnp.int32, (128, 128), 0)
        c = lax.broadcasted_iota(jnp.int32, (128, 128), 1)
        upper = jnp.where(r <= c, 1.0, 0.0).astype(BF)
        before = jnp.full((PLANES, 1), -1.0, F32)
        for lo in range(0, tok, 128):
            part = live[:, lo : lo + 128]
            rank = dot(part.astype(BF), upper, 1, 0) + before
            pos = jnp.where(part > 0.0, rank, -float(slots))
            pos_s[:, lo : lo + 128] = pos.astype(jnp.int32)
            post_s[lo : lo + 128, :] = pos.T
            before = before + jnp.sum(part, axis=1, keepdims=True)
        for j in range(NX):
            hit = pos_s[j : j + 1, :] == slot
            sel_s[j * SLOTS : (j + 1) * SLOTS, :] = jnp.where(hit, 1.0, 0.0).astype(BF)
        for lo in range(0, feat, 512):
            span = slice(lo, lo + 512)
            xe_s[:, span] = dot(sel_s[...], xa_ref[:, span], 1, 0).astype(BF)
            de_s[:, span] = dot(sel_s[...], xb_ref[:, span], 1, 0).astype(BF)

    here = pl.ds(pl.multiple_of(e * SLOTS, SLOTS), SLOTS)
    xe = xe_s[here, :]
    de = de_s[here, :]
    picked = pos_s[pl.ds(e, 1), :] == slot
    w = jnp.sum(jnp.where(picked, w_s[pl.ds(e, 1), :], 0.0), axis=1, keepdims=True)
    wt = wt_ref[:, 0].reshape(feat, 3 * hid)
    gu = dot(xe, wt[:, : 2 * hid], 1, 0)
    hd = dot(de, wt[:, 2 * hid :], 1, 0)
    g = gu[:, :hid]
    u = gu[:, hid:]
    s = jax.nn.sigmoid(g)
    gs = g * s
    h = gs * u
    rg = jnp.sum(h * hd, axis=1, keepdims=True)
    wh = (w * h).astype(BF)
    hg = w * hd
    gb = (hg * u * s * (1.0 + g * (1.0 - s))).astype(BF)
    ub = (hg * gs).astype(BF)
    act = jnp.concatenate([gb, ub], axis=1)
    rows_s[here, :feat] = dot(wh, wt[:, 2 * hid :], 1, 1).astype(BF)
    lane = lax.broadcasted_iota(jnp.int32, (SLOTS, AUX), 1)
    mine = col + e
    rg_hi = rg.astype(BF).astype(F32)
    aux = jnp.where(lane == mine, rg_hi, 0.0) + jnp.where(lane == mine + AUX // 2, rg - rg_hi, 0.0)
    rows_s[here, feat : feat + AUX] = aux.astype(BF)
    rows_s[here, feat + AUX :] = dot(act, wt[:, : 2 * hid], 1, 1).astype(BF)
    step = feat // NDP

    def halves(v):
        even = jnp.concatenate([v[:, i * step : (i + 1) * step] for i in range(0, NDP, 2)], axis=1)
        odd = jnp.concatenate([v[:, i * step : (i + 1) * step] for i in range(1, NDP, 2)], axis=1)
        return jnp.where(core == 0, even, odd), jnp.where(core == 0, odd, even)

    xk, xs = halves(xe)
    dk, ds = halves(de)
    keep_ref[:, 0, :, : 2 * hid] = dot(xk, act, 0, 0).astype(BF).reshape(NY, step, 2 * hid)
    keep_ref[:, 0, :, 2 * hid :] = dot(dk, wh, 0, 0).astype(BF).reshape(NY, step, hid)
    send_ref[:, 0, :, : 2 * hid] = dot(xs, act, 0, 0).astype(BF).reshape(NY, step, 2 * hid)
    send_ref[:, 0, :, 2 * hid :] = dot(ds, wh, 0, 0).astype(BF).reshape(NY, step, hid)

    quarter = tok // NX
    for part in range(0, quarter, MERGE):
        span = pl.ds(pl.multiple_of(e * quarter + part, MERGE), MERGE)
        lane = lax.broadcasted_iota(jnp.int32, (MERGE, slots), 1).astype(F32)
        sel = jnp.zeros((MERGE, slots), F32)
        for j in range(NX):
            sel = jnp.where(post_s[span, j : j + 1] + float(j * SLOTS) == lane, 1.0, sel)
        selt_s[span, :] = sel.astype(BF)

    @pl.when(e == NX - 1)
    def _():
        for lo, hi in ((0, feat // 2), (feat // 2, feat), (feat, feat + AUX)):
            pa_ref[:, lo:hi] = dot(selt_s[...], rows_s[:, lo:hi], 1, 0).astype(BF)
        for lo in range(0, feat, feat // 2):
            off = feat + AUX + lo
            rows = rows_s[:, off : off + feat // 2]
            pb_ref[:, lo : lo + feat // 2] = dot(selt_s[...], rows, 1, 0).astype(BF)


def experts(ids, xa, xb, wt):
    tok, feat = xb.shape
    hid3 = wt.shape[3]
    rows = feat // NDP
    slots = NX * SLOTS
    width = 2 * feat + AUX
    flops = 2 * slots * (tok * width * 2 + 9 * feat * hid3 // 3)
    whole = lambda e, s: (0, 0)
    return pl.pallas_call(
        moe_kernel,
        grid_spec=pltpu.PrefetchScalarGridSpec(
            num_scalar_prefetch=1,
            grid=(NX,),
            in_specs=[
                pl.BlockSpec((tok, feat + AUX), whole),
                pl.BlockSpec((tok, feat), whole),
                pl.BlockSpec((NDP, 1, rows, hid3), lambda e, s: (0, e, 0, 0)),
            ],
            out_specs=[
                pl.BlockSpec((NY, 1, rows, hid3), lambda e, s: (0, e, 0, 0)),
                pl.BlockSpec((NY, 1, rows, hid3), lambda e, s: (0, e, 0, 0)),
                pl.BlockSpec((tok, feat + AUX), whole),
                pl.BlockSpec((tok, feat), whole),
            ],
            scratch_shapes=[
                pltpu.VMEM((PLANES, tok), jnp.int32),
                pltpu.VMEM((tok, PLANES), F32),
                pltpu.VMEM((PLANES, tok), F32),
                pltpu.VMEM((slots, tok), BF),
                pltpu.VMEM((tok, slots), BF),
                pltpu.VMEM((slots, feat), BF),
                pltpu.VMEM((slots, feat), BF),
                pltpu.VMEM((slots, width), BF),
            ],
        ),
        out_shape=[
            jax.ShapeDtypeStruct((NY, NX, rows, hid3), BF),
            jax.ShapeDtypeStruct((NY, NX, rows, hid3), BF),
            jax.ShapeDtypeStruct((tok, feat + AUX), BF),
            jax.ShapeDtypeStruct((tok, feat), BF),
        ],
        cost_estimate=pl.CostEstimate(
            flops=flops, bytes_accessed=30_000_000, transcendentals=slots * hid3 // 3
        ),
    )(ids, xa, xb, wt)


def pack_kernel(g_ref, u_ref, d_ref, o_ref):
    hid = g_ref.shape[2]
    o_ref[:, :hid] = g_ref[0]
    o_ref[:, hid : 2 * hid] = u_ref[0]
    o_ref[:, 2 * hid :] = d_ref[0].astype(F32).T.astype(BF)


def pack(g, u, d):
    return pl.pallas_call(
        pack_kernel, out_shape=jax.ShapeDtypeStruct((g.shape[1], 3 * g.shape[2]), BF)
    )(g, u, d)


def unpack_kernel(s_ref, g_ref, u_ref, d_ref):
    hid = g_ref.shape[2]
    g_ref[0] = s_ref[:, :hid].astype(F32)
    u_ref[0] = s_ref[:, hid : 2 * hid].astype(F32)
    d_ref[0] = s_ref[:, 2 * hid :].astype(F32).T


def unpack(s):
    rows, hid = s.shape[0], s.shape[1] // 3
    return pl.pallas_call(
        unpack_kernel,
        out_shape=[
            jax.ShapeDtypeStruct((1, rows, hid), F32),
            jax.ShapeDtypeStruct((1, rows, hid), F32),
            jax.ShapeDtypeStruct((1, hid, rows), F32),
        ],
    )(s)


def around(value, sign, far=False):
    pairs = [(NZ + z, NZ + (z - sign) % NZ) for z in range(NZ)]
    if not far:
        pairs += [(z, (z + sign) % NZ) for z in range(NZ)]
    return lax.ppermute(value, ("c", "z"), pairs)


def swap(value):
    return lax.ppermute(value, "c", [(0, 1), (1, 0)])


def add(a, b):
    return (a.astype(F32) + b.astype(F32)).astype(BF)


def shards(tokens, expert_ids, route_weight, out_grad, gate_weight, up_weight, down_weight):
    rows, feat = tokens.shape
    hid = gate_weight.shape[2]
    z = lax.axis_index("z").astype(jnp.int32)
    core = lax.axis_index("c").astype(jnp.int32)
    half = AUX // 2
    pair_rows = 2 * rows
    wa = lax.all_gather(pack(gate_weight, up_weight, down_weight), ("y", "c", "x"), axis=0, tiled=True)
    place = (expert_ids % NZ) * NX + expert_ids // NZ
    hot = place[:, :, None] == jnp.arange(half, dtype=jnp.int32)
    dense = jnp.sum(jnp.where(hot, route_weight[:, :, None], 0.0), 1)
    hi = lax.reduce_precision(dense, 8, 7)
    own_a = jnp.concatenate([tokens, hi.astype(BF), (dense - hi).astype(BF)], axis=1)
    chain_a = chip_a = jnp.concatenate([own_a, swap(own_a)], axis=0)
    chain_b = chip_b = jnp.concatenate([out_grad, swap(out_grad)], axis=0)
    got_a, got_b = [], []
    for hop in range(1, HOPS + 1):
        chain_a = around(chain_a, 1, hop == HOPS)
        chain_b = around(chain_b, 1, hop == HOPS)
        got_a.append(chain_a)
        got_b.append(chain_b)
    got_a[-1] = jnp.where(core == 0, chip_a, got_a[-1])
    got_b[-1] = jnp.where(core == 0, chip_b, got_b[-1])
    keep, send, pa, pb = experts(
        jnp.stack([z * NX, core]),
        jnp.concatenate(got_a, axis=0),
        jnp.concatenate(got_b, axis=0),
        wa.reshape(NDP, NX, feat // NDP, 3 * hid),
    )
    grads = add(keep, swap(send))
    summed = lax.psum_scatter(
        grads.reshape(-1, 3 * hid), ("y", "x"), scatter_dimension=0, tiled=True
    )

    def block(part, hop):
        return part[(hop - 1) * pair_rows : hop * pair_rows]

    none = jnp.zeros((), BF)
    chain_a = block(pa, HOPS)
    chain_b = block(pb, HOPS)
    for hop in range(HOPS, 0, -1):
        chain_a = around(chain_a, -1, hop == HOPS)
        chain_b = around(chain_b, -1, hop == HOPS)
        if hop > 1:
            chain_a = add(chain_a, block(pa, hop - 1))
            chain_b = add(chain_b, block(pb, hop - 1))
    chain_a = add(chain_a, jnp.where(core == 0, block(pa, HOPS), none))
    chain_b = add(chain_b, jnp.where(core == 0, block(pb, HOPS), none))
    total_a = chain_a[:rows].astype(F32) + swap(chain_a[rows:]).astype(F32)
    total_b = chain_b[:rows].astype(F32) + swap(chain_b[rows:]).astype(F32)
    layer_out = total_a[:, :feat].astype(BF)
    token_grad = total_b.astype(BF)
    pair = total_a[:, feat : feat + half] + total_a[:, feat + half :]
    route_grad = jnp.sum(jnp.where(hot, pair[:, None, :], 0.0), 2)
    return (layer_out, token_grad, route_grad, *unpack(summed))


def solution(mesh):
    grid = Mesh(mesh.devices.reshape(NY, NC, NX, NZ), ("y", "c", "x", "z"))
    dp, ex = ("y", "c"), ("x", "z")
    rowwise = P(dp + ex, None)
    weights = (P(ex, dp, None), P(ex, dp, None), P(ex, None, dp))
    return jax.shard_map(
        shards,
        mesh=grid,
        in_specs=(rowwise, rowwise, rowwise, rowwise, *weights),
        out_specs=(rowwise, rowwise, rowwise, *weights),
        check_vma=False,
    )
```

```python
import jax
import jax.numpy as jnp
from jax import lax
from jax.experimental import pallas as pl
from jax.experimental.pallas import tpu as pltpu
from jax.sharding import Mesh
from jax.sharding import PartitionSpec as P

BF = jnp.bfloat16
F32 = jnp.float32
NX, NY, NZ, NC = 4, 4, 16, 2
NDP = NY * NC
HOPS = NZ // 2
CAP = 10
SLOTS = NZ * CAP
AUX = 128
PLANES = 8
MERGE = 64


def dot(a, b, ca, cb):
    return lax.dot_general(a, b, (((ca,), (cb,)), ((), ())), preferred_element_type=F32)


def moe_kernel(ids_ref, xa_ref, xb_ref, wt_ref, keep_ref, send_ref, rows_ref, selt_ref, pos_s, post_s, w_s, sel_s, xe_s, de_s):
    e = pl.program_id(0)
    col = ids_ref[0]
    core = ids_ref[1]
    tok = xa_ref.shape[0]
    feat = xb_ref.shape[1]
    hid = wt_ref.shape[3] // 3
    slots = NX * SLOTS
    slot = lax.broadcasted_iota(jnp.int32, (SLOTS, tok), 0)

    @pl.when(e == 0)
    def _():
        row = lax.broadcasted_iota(jnp.int32, (PLANES, AUX), 0)
        lane = lax.broadcasted_iota(jnp.int32, (PLANES, AUX), 1)
        want = (row < NX) & ((lane == col + row) | (lane == col + row + AUX // 2))
        w = dot(jnp.where(want, 1.0, 0.0).astype(BF), xa_ref[:, feat:], 1, 1)
        w_s[...] = w
        live = jnp.where(w > 0.0, 1.0, 0.0)
        r = lax.broadcasted_iota(jnp.int32, (128, 128), 0)
        c = lax.broadcasted_iota(jnp.int32, (128, 128), 1)
        upper = jnp.where(r <= c, 1.0, 0.0).astype(BF)
        before = jnp.full((PLANES, 1), -1.0, F32)
        for lo in range(0, tok, 128):
            part = live[:, lo : lo + 128]
            rank = dot(part.astype(BF), upper, 1, 0) + before
            pos = jnp.where(part > 0.0, rank, -float(slots))
            pos_s[:, lo : lo + 128] = pos.astype(jnp.int32)
            post_s[lo : lo + 128, :] = pos.T
            before = before + jnp.sum(part, axis=1, keepdims=True)
        for j in range(NX):
            hit = pos_s[j : j + 1, :] == slot
            sel_s[j * SLOTS : (j + 1) * SLOTS, :] = jnp.where(hit, 1.0, 0.0).astype(BF)
        for lo in range(0, feat, 512):
            span = slice(lo, lo + 512)
            xe_s[:, span] = dot(sel_s[...], xa_ref[:, span], 1, 0).astype(BF)
            de_s[:, span] = dot(sel_s[...], xb_ref[:, span], 1, 0).astype(BF)

    here = pl.ds(pl.multiple_of(e * SLOTS, SLOTS), SLOTS)
    xe = xe_s[here, :]
    de = de_s[here, :]
    picked = pos_s[pl.ds(e, 1), :] == slot
    w = jnp.sum(jnp.where(picked, w_s[pl.ds(e, 1), :], 0.0), axis=1, keepdims=True)
    wt = wt_ref[:, 0].reshape(feat, 3 * hid)
    gu = dot(xe, wt[:, : 2 * hid], 1, 0)
    hd = dot(de, wt[:, 2 * hid :], 1, 0)
    g = gu[:, :hid]
    u = gu[:, hid:]
    s = jax.nn.sigmoid(g)
    gs = g * s
    h = gs * u
    rg = jnp.sum(h * hd, axis=1, keepdims=True)
    wh = (w * h).astype(BF)
    hg = w * hd
    gb = (hg * u * s * (1.0 + g * (1.0 - s))).astype(BF)
    ub = (hg * gs).astype(BF)
    act = jnp.concatenate([gb, ub], axis=1)
    rows_ref[:, :feat] = dot(wh, wt[:, 2 * hid :], 1, 1).astype(BF)
    lane = lax.broadcasted_iota(jnp.int32, (SLOTS, AUX), 1)
    mine = col + e
    rg_hi = rg.astype(BF).astype(F32)
    aux = jnp.where(lane == mine, rg_hi, 0.0) + jnp.where(lane == mine + AUX // 2, rg - rg_hi, 0.0)
    rows_ref[:, feat : feat + AUX] = aux.astype(BF)
    rows_ref[:, feat + AUX :] = dot(act, wt[:, : 2 * hid], 1, 1).astype(BF)
    step = feat // NDP

    def halves(v):
        even = jnp.concatenate([v[:, i * step : (i + 1) * step] for i in range(0, NDP, 2)], axis=1)
        odd = jnp.concatenate([v[:, i * step : (i + 1) * step] for i in range(1, NDP, 2)], axis=1)
        return jnp.where(core == 0, even, odd), jnp.where(core == 0, odd, even)

    xk, xs = halves(xe)
    dk, ds = halves(de)
    keep_ref[:, 0, :, : 2 * hid] = dot(xk, act, 0, 0).astype(BF).reshape(NY, step, 2 * hid)
    keep_ref[:, 0, :, 2 * hid :] = dot(dk, wh, 0, 0).astype(BF).reshape(NY, step, hid)
    send_ref[:, 0, :, : 2 * hid] = dot(xs, act, 0, 0).astype(BF).reshape(NY, step, 2 * hid)
    send_ref[:, 0, :, 2 * hid :] = dot(ds, wh, 0, 0).astype(BF).reshape(NY, step, hid)

    quarter = tok // NX
    for part in range(0, quarter, MERGE):
        span = pl.ds(pl.multiple_of(e * quarter + part, MERGE), MERGE)
        lane = lax.broadcasted_iota(jnp.int32, (MERGE, slots), 1).astype(F32)
        sel = jnp.zeros((MERGE, slots), F32)
        for j in range(NX):
            sel = jnp.where(post_s[span, j : j + 1] + float(j * SLOTS) == lane, 1.0, sel)
        selt_ref[part : part + MERGE, :] = sel.astype(BF)


def merge_kernel(rows_ref, selt_ref, pa_ref, pb_ref):
    feat = pb_ref.shape[1]
    for lo, hi in ((0, feat // 2), (feat // 2, feat), (feat, feat + AUX)):
        pa_ref[:, lo:hi] = dot(selt_ref[...], rows_ref[:, lo:hi], 1, 0).astype(BF)
    for lo in range(0, feat, feat // 2):
        off = feat + AUX + lo
        rows = rows_ref[:, off : off + feat // 2]
        pb_ref[:, lo : lo + feat // 2] = dot(selt_ref[...], rows, 1, 0).astype(BF)


def merge(rows, selt):
    slots, width = rows.shape
    tok = selt.shape[0]
    feat = (width - AUX) // 2
    return pl.pallas_call(
        merge_kernel,
        out_shape=[
            jax.ShapeDtypeStruct((tok, feat + AUX), BF),
            jax.ShapeDtypeStruct((tok, feat), BF),
        ],
        cost_estimate=pl.CostEstimate(
            flops=2 * slots * tok * width, bytes_accessed=9_000_000, transcendentals=0
        ),
    )(rows, selt)


def experts(ids, xa, xb, wt):
    tok, feat = xb.shape
    hid3 = wt.shape[3]
    rows = feat // NDP
    slots = NX * SLOTS
    width = 2 * feat + AUX
    flops = 2 * slots * (tok * width * 2 + 9 * feat * hid3 // 3)
    whole = lambda e, s: (0, 0)
    return pl.pallas_call(
        moe_kernel,
        grid_spec=pltpu.PrefetchScalarGridSpec(
            num_scalar_prefetch=1,
            grid=(NX,),
            in_specs=[
                pl.BlockSpec((tok, feat + AUX), whole),
                pl.BlockSpec((tok, feat), whole),
                pl.BlockSpec((NDP, 1, rows, hid3), lambda e, s: (0, e, 0, 0)),
            ],
            out_specs=[
                pl.BlockSpec((NY, 1, rows, hid3), lambda e, s: (0, e, 0, 0)),
                pl.BlockSpec((NY, 1, rows, hid3), lambda e, s: (0, e, 0, 0)),
                pl.BlockSpec((SLOTS, width), lambda e, s: (e, 0)),
                pl.BlockSpec((tok // NX, slots), lambda e, s: (e, 0)),
            ],
            scratch_shapes=[
                pltpu.VMEM((PLANES, tok), jnp.int32),
                pltpu.VMEM((tok, PLANES), F32),
                pltpu.VMEM((PLANES, tok), F32),
                pltpu.VMEM((slots, tok), BF),
                pltpu.VMEM((slots, feat), BF),
                pltpu.VMEM((slots, feat), BF),
            ],
        ),
        out_shape=[
            jax.ShapeDtypeStruct((NY, NX, rows, hid3), BF),
            jax.ShapeDtypeStruct((NY, NX, rows, hid3), BF),
            jax.ShapeDtypeStruct((slots, width), BF),
            jax.ShapeDtypeStruct((tok, slots), BF),
        ],
        cost_estimate=pl.CostEstimate(
            flops=flops, bytes_accessed=30_000_000, transcendentals=slots * hid3 // 3
        ),
    )(ids, xa, xb, wt)


def pack_kernel(g_ref, u_ref, d_ref, o_ref):
    hid = g_ref.shape[2]
    o_ref[:, :hid] = g_ref[0]
    o_ref[:, hid : 2 * hid] = u_ref[0]
    o_ref[:, 2 * hid :] = d_ref[0].astype(F32).T.astype(BF)


def pack(g, u, d):
    return pl.pallas_call(
        pack_kernel, out_shape=jax.ShapeDtypeStruct((g.shape[1], 3 * g.shape[2]), BF)
    )(g, u, d)


def unpack_kernel(s_ref, g_ref, u_ref, d_ref):
    hid = g_ref.shape[2]
    g_ref[0] = s_ref[:, :hid].astype(F32)
    u_ref[0] = s_ref[:, hid : 2 * hid].astype(F32)
    d_ref[0] = s_ref[:, 2 * hid :].astype(F32).T


def unpack(s):
    rows, hid = s.shape[0], s.shape[1] // 3
    return pl.pallas_call(
        unpack_kernel,
        out_shape=[
            jax.ShapeDtypeStruct((1, rows, hid), F32),
            jax.ShapeDtypeStruct((1, rows, hid), F32),
            jax.ShapeDtypeStruct((1, hid, rows), F32),
        ],
    )(s)


def around(value, sign, far=False):
    pairs = [(NZ + z, NZ + (z - sign) % NZ) for z in range(NZ)]
    if not far:
        pairs += [(z, (z + sign) % NZ) for z in range(NZ)]
    return lax.ppermute(value, ("c", "z"), pairs)


def swap(value):
    return lax.ppermute(value, "c", [(0, 1), (1, 0)])


def add(a, b):
    return (a.astype(F32) + b.astype(F32)).astype(BF)


def shards(tokens, expert_ids, route_weight, out_grad, gate_weight, up_weight, down_weight):
    rows, feat = tokens.shape
    hid = gate_weight.shape[2]
    z = lax.axis_index("z").astype(jnp.int32)
    core = lax.axis_index("c").astype(jnp.int32)
    half = AUX // 2
    pair_rows = 2 * rows
    wa = lax.all_gather(pack(gate_weight, up_weight, down_weight), ("y", "c", "x"), axis=0, tiled=True)
    place = (expert_ids % NZ) * NX + expert_ids // NZ
    hot = place[:, :, None] == jnp.arange(half, dtype=jnp.int32)
    dense = jnp.sum(jnp.where(hot, route_weight[:, :, None], 0.0), 1)
    hi = lax.reduce_precision(dense, 8, 7)
    own_a = jnp.concatenate([tokens, hi.astype(BF), (dense - hi).astype(BF)], axis=1)
    chain_a = chip_a = jnp.concatenate([own_a, swap(own_a)], axis=0)
    chain_b = chip_b = jnp.concatenate([out_grad, swap(out_grad)], axis=0)
    got_a, got_b = [], []
    for hop in range(1, HOPS + 1):
        chain_a = around(chain_a, 1, hop == HOPS)
        chain_b = around(chain_b, 1, hop == HOPS)
        got_a.append(chain_a)
        got_b.append(chain_b)
    got_a[-1] = jnp.where(core == 0, chip_a, got_a[-1])
    got_b[-1] = jnp.where(core == 0, chip_b, got_b[-1])
    keep, send, *saved = experts(
        jnp.stack([z * NX, core]),
        jnp.concatenate(got_a, axis=0),
        jnp.concatenate(got_b, axis=0),
        wa.reshape(NDP, NX, feat // NDP, 3 * hid),
    )
    send = swap(send)
    pa, pb = merge(*saved)
    grads = add(keep, send)
    summed = lax.psum_scatter(
        grads.reshape(-1, 3 * hid), ("y", "x"), scatter_dimension=0, tiled=True
    )

    def block(part, hop):
        return part[(hop - 1) * pair_rows : hop * pair_rows]

    none = jnp.zeros((), BF)
    chain_a = block(pa, HOPS)
    chain_b = block(pb, HOPS)
    for hop in range(HOPS, 0, -1):
        chain_a = around(chain_a, -1, hop == HOPS)
        chain_b = around(chain_b, -1, hop == HOPS)
        if hop > 1:
            chain_a = add(chain_a, block(pa, hop - 1))
            chain_b = add(chain_b, block(pb, hop - 1))
    chain_a = add(chain_a, jnp.where(core == 0, block(pa, HOPS), none))
    chain_b = add(chain_b, jnp.where(core == 0, block(pb, HOPS), none))
    total_a = chain_a[:rows].astype(F32) + swap(chain_a[rows:]).astype(F32)
    total_b = chain_b[:rows].astype(F32) + swap(chain_b[rows:]).astype(F32)
    layer_out = total_a[:, :feat].astype(BF)
    token_grad = total_b.astype(BF)
    pair = total_a[:, feat : feat + half] + total_a[:, feat + half :]
    route_grad = jnp.sum(jnp.where(hot, pair[:, None, :], 0.0), 2)
    return (layer_out, token_grad, route_grad, *unpack(summed))


def solution(mesh):
    grid = Mesh(mesh.devices.reshape(NY, NC, NX, NZ), ("y", "c", "x", "z"))
    dp, ex = ("y", "c"), ("x", "z")
    rowwise = P(dp + ex, None)
    weights = (P(ex, dp, None), P(ex, dp, None), P(ex, None, dp))
    return jax.shard_map(
        shards,
        mesh=grid,
        in_specs=(rowwise, rowwise, rowwise, rowwise, *weights),
        out_specs=(rowwise, rowwise, rowwise, *weights),
        check_vma=False,
    )
```
